256 devices in a mesh: slab: 8 (over y, core), front: 32 (over z, x).
Axes of the slice: x: 4, y: 4, z: 8, core: 2. Of those that a mesh axis runs over, the one named last changes fastest.
Arguments:
- source: bfloat16 [8, 32, 2, 768, 128], P('slab', 'front'), may hold values from -6 to 6
- leaf_inverse: bfloat16 [8, 32, 2, 768, 768], P('slab', 'front'), may hold values from -0.15625 to 0.15625
- boundary_map: bfloat16 [8, 32, 2, 384, 768], P('slab', 'front'), may hold values from -0.15625 to 0.15625
- sep_inverse: bfloat16 [8, 96, 2, 384, 384], P('slab', 'front'), may hold values from -0.4375 to 0.4375
- owner_map: int32 [8, 64], P('slab'), may hold values from 0 to 31, as said below
- piece_count: int32 [8, 32], P('slab', 'front'), may hold values from 18 to 24, as said below
- piece_target: int32 [8, 32, 24], P('slab', 'front'), may hold values from 0 to 1535, as said below
Outputs:
- solution: bfloat16 [8, 32, 2, 768, 128], P('slab', 'front')
- trace: bfloat16 [8, 32, 24, 2, 16, 128], P('slab', 'front')
The draws below stay inside these ranges and needn't reach their ends.
Inputs may be any that keep to these rules, and one draw needn't show every extreme that they name: `owner_map`: every owner holds 1 or 3 separators; a fraction 1 / 2 of the owners hold 3. `piece_count`: in every slab one leaf uses all its blocks. `piece_target`: entry j * 24 + q names part q of separator j. The used blocks of the leaves of one device name separators of one owner at most 2 times; in every slab some owner receives exactly 2 used blocks from every device.
All inputs are finite; a program needn't handle non-finite values.
Results may differ from the reference program's by a relative error of at most 0.025.
Values may be sent and summed in bfloat16 or wider, within the bound.
A program may use at most 128 MiB of HBM per device.

```python
import jax
import jax.numpy as jnp

INTERIOR = 768
BND = 384
PIECE_ROWS = 16
SEPW = 384
LEAVES = 1
SLOTS = 3
COLS = 64
PIECES = 24
PARTS_SIZE = 24
SLABS = 8
NSEP = 64
N_FRONT = 32


def routing(key):
    base = jax.random.fold_in(key, 11)
    key_own, key_dest, key_star, key_slot, key_part, key_count = jax.random.split(base, 6)
    front_size = NSEP // 2
    busy_count = front_size // (SLOTS - 1)
    own_perm = jax.vmap(lambda one_key: jax.random.permutation(one_key, front_size))(jax.random.split(key_own, SLABS)).astype(jnp.int32)
    sep_ids = jnp.arange(NSEP, dtype=jnp.int32)
    column = jnp.where(sep_ids < front_size, sep_ids, (sep_ids - front_size) // (SLOTS - 1))
    owner_table = own_perm[:, column]
    inverse_perm = jnp.argsort(own_perm, axis=1, stable=True).astype(jnp.int32)
    dest_keys = jax.random.split(key_dest, SLABS * front_size)
    dest_perm = jax.vmap(lambda one_key: jax.random.permutation(one_key, front_size))(dest_keys).astype(jnp.int32)
    dest_perm = dest_perm.reshape(SLABS, front_size, front_size)
    star = jax.random.randint(key_star, (SLABS,), 0, front_size).astype(jnp.int32)
    star_full = star[:, None, None]
    leading = dest_perm[:, :, :1]
    place = jnp.arange(front_size, dtype=jnp.int32)[None, None, :]
    dest_perm = jnp.where(place == 0, star_full, jnp.where(dest_perm == star_full, leading, dest_perm))
    total = LEAVES * PIECES
    pair_ids = jnp.arange(total, dtype=jnp.int32) // 2 % front_size
    destination = dest_perm[:, :, pair_ids]
    inverse_full = jnp.broadcast_to(inverse_perm[:, None, :], (SLABS, front_size, front_size))
    owner_place = jnp.take_along_axis(inverse_full, destination, axis=2)
    load = jnp.where(owner_place < busy_count, SLOTS, 1)
    chosen = jax.random.randint(key_slot, destination.shape, 0, 1 << 20).astype(jnp.int32) % load
    separator = jnp.where(chosen == 0, owner_place, front_size + (SLOTS - 1) * owner_place + chosen - 1)
    part_pick = jax.random.randint(key_part, destination.shape, 0, PARTS_SIZE).astype(jnp.int32)
    targets = (separator * PARTS_SIZE + part_pick).reshape(SLABS, front_size * LEAVES, PIECES).astype(jnp.int32)
    counts = jax.random.randint(key_count, (SLABS, front_size * LEAVES), PIECES * 3 // 4, PIECES + 1).astype(jnp.int32)
    counts = counts.at[:, 0].set(PIECES)
    return (owner_table.astype(jnp.int32), counts, targets)


def draw_owner_map(key, part):
    return routing(key)[0]


def draw_piece_count(key, part):
    return routing(key)[1]


def draw_piece_target(key, part):
    return routing(key)[2]


def steps_of(stream_key, shape, cuts, low, top_value):
    loudness, own = 1.0, jax.random.fold_in(stream_key, 6)
    for axis_at, parts in cuts:
        steps = jnp.exp(jax.random.uniform(jax.random.fold_in(own, axis_at), (parts,), jnp.float32, low / len(cuts), top_value / len(cuts)))
        loudness = loudness * jnp.repeat(steps, shape[axis_at] // parts).reshape([-1 if axis == axis_at else 1 for axis in range(len(shape))])
    return loudness


def bell_draw(stream_key, shape, spread, limit, cuts=(), kind=jnp.bfloat16):
    factor_of = steps_of(stream_key, shape, cuts, -0.22, 0.18) if cuts else 1.0
    drawn = jax.random.normal(stream_key, shape, jnp.float32) * spread * factor_of
    return jnp.minimum(jnp.maximum(drawn, -limit), limit).astype(kind)


def setup_inputs(seed: int = 0) -> dict:
    keys = jax.random.split(jax.random.key(seed), 8)
    source = bell_draw(keys[0], (SLABS, N_FRONT * LEAVES, 2, INTERIOR, 2 * COLS), 1.0, 6.0, ((0, 8), (1, 32)))
    leaf_inverse = bell_draw(keys[1], (SLABS, N_FRONT * LEAVES, 2, INTERIOR, INTERIOR), (2 * INTERIOR) ** -0.5, 0.15625, ((0, 8), (1, 32)))
    boundary_map = bell_draw(keys[2], (SLABS, N_FRONT * LEAVES, 2, BND, INTERIOR), (2 * INTERIOR) ** -0.5, 0.15625, ((0, 8), (1, 32)))
    sep_inverse = bell_draw(keys[3], (SLABS, N_FRONT * SLOTS, 2, SEPW, SEPW), (BND * BND // INTERIOR) ** -0.5, 0.4375, ((0, 8), (1, 32)))
    owner_map = draw_owner_map(jax.random.fold_in(keys[7], 71), 0)
    piece_count = draw_piece_count(jax.random.fold_in(keys[7], 71), 0)
    piece_target = draw_piece_target(jax.random.fold_in(keys[7], 71), 0)
    return dict(source=source, leaf_inverse=leaf_inverse, boundary_map=boundary_map, sep_inverse=sep_inverse, owner_map=owner_map, piece_count=piece_count, piece_target=piece_target)


def capply(mat, vec):
    mat = mat.astype(jnp.float32)
    vec = vec.astype(jnp.float32)

    def mult(left, right):
        return jnp.einsum("bnm,bmc->bnc", left, right)

    real_part = mult(mat[:, 0], vec[:, 0]) - mult(mat[:, 1], vec[:, 1])
    imag_part = mult(mat[:, 0], vec[:, 1]) + mult(mat[:, 1], vec[:, 0])
    return jnp.stack([real_part, imag_part], axis=1)


def reference(source, leaf_inverse, boundary_map, sep_inverse, owner_map, piece_count, piece_target):
    leaf_total = source.shape[1]
    columns = source.shape[-1]
    trace = jnp.zeros((leaf_total, PIECES, 2, PIECE_ROWS, columns), jnp.bfloat16)
    solutions = []
    traces = []
    for slab in range(SLABS):
        incoming = trace.transpose(0, 2, 1, 3, 4).reshape(leaf_total, 2, BND, columns).astype(jnp.float32)
        padded = jnp.pad(incoming, ((0, 0), (0, 0), (0, INTERIOR - BND), (0, 0)))
        rhs_total = source[slab].astype(jnp.float32) + padded
        solution = capply(leaf_inverse[slab], rhs_total).astype(jnp.bfloat16)
        resid = capply(boundary_map[slab], solution).astype(jnp.bfloat16)
        blocks = resid.reshape(leaf_total, 2, PIECES, PIECE_ROWS, columns).transpose(0, 2, 1, 3, 4)
        blocks = blocks.reshape(leaf_total * PIECES, 2, PIECE_ROWS, columns)
        usable = (jnp.arange(PIECES, dtype=jnp.int32)[None, :] < piece_count[slab][:, None]).reshape(-1)
        flat_target = piece_target[slab].reshape(-1).astype(jnp.int32)
        data = jnp.where(usable[:, None, None, None], blocks.astype(jnp.float32), jnp.zeros((), jnp.float32))
        summed = jax.ops.segment_sum(data, flat_target, num_segments=NSEP * PARTS_SIZE)
        summed = summed.reshape(NSEP, PARTS_SIZE, 2, PIECE_ROWS, columns).transpose(0, 2, 1, 3, 4)
        summed = summed.reshape(NSEP, 2, SEPW, columns).astype(jnp.bfloat16)
        owners = owner_map[slab].astype(jnp.int32)
        sep_ids = jnp.arange(NSEP, dtype=jnp.int32)
        earlier = (owners[:, None] == owners[None, :]) & (sep_ids[:, None] > sep_ids[None, :])
        slot_of = jnp.sum(jnp.where(earlier, 1, 0), axis=1).astype(jnp.int32)
        inverses = sep_inverse[slab][(owners * SLOTS + slot_of).astype(jnp.int32)]
        values = capply(inverses, summed).astype(jnp.bfloat16)
        positions = values.reshape(NSEP, 2, PARTS_SIZE, PIECE_ROWS, columns).transpose(0, 2, 1, 3, 4)
        positions = positions.reshape(NSEP * PARTS_SIZE, 2, PIECE_ROWS, columns)
        picked = jnp.where(usable[:, None, None, None], positions[flat_target], jnp.zeros((), jnp.bfloat16))
        trace = picked.reshape(leaf_total, PIECES, 2, PIECE_ROWS, columns)
        solutions.append(solution)
        traces.append(trace)
    return jnp.stack(solutions), jnp.stack(traces)
```

```python
import functools

import jax
import jax.numpy as jnp
from jax import lax
from jax.experimental import pallas as pl
from jax.experimental.pallas import tpu as pltpu
from jax.sharding import PartitionSpec as P

MESH = pl.DeviceIdType.MESH
BF16 = jnp.bfloat16
F32 = jnp.float32
LANES = 128


def mm(a, b):
    return jnp.dot(a, b, preferred_element_type=F32)


def sweep_kernel(
    slabs,
    fronts,
    ring,
    src_ref,
    inv_hbm,
    cpl_hbm,
    sep_hbm,
    tab_ref,
    tab_smem,
    sol_ref,
    trace_ref,
    leaf2,
    cpl2,
    sep2,
    comp2,
    xs,
    xb,
    xin,
    xsep,
    base,
    resid0,
    rblk,
    inc,
    out_a,
    recv_a,
    run,
    vals,
    out_b,
    recv_b,
    recv_t,
    home,
    tag_recv,
    tab_recv,
    own_tab,
    own_smem,
    prev_smem,
    load_sem,
    sep_sem,
    tag_send,
    tag_arrive,
    prev_send,
    prev_arrive,
    a_send,
    a_arrive,
    b_send,
    b_arrive,
    t_arrive,
    home_send,
    home_arrive,
    smem_sem,
):
    s = lax.axis_index("slab")
    f = lax.axis_index("front")
    last = slabs - 1
    interior, cols = src_ref.shape[1], src_ref.shape[2]
    bnd = cpl2.shape[0]
    slots, sepw = sep2.shape[0], sep2.shape[1]
    pieces = inc.shape[0]
    rows = inc.shape[2]
    parts = sepw // rows
    positions = slots * parts
    cap = 2 * fronts
    halves = interior // bnd
    depth = fronts // ring

    def peer(i):
        j, k = i // ring, i % ring
        dz = depth // 2 + (1 - 2 * (j % 2)) * ((j + 1) // 2)
        dx = ring // 2 + (1 - 2 * (k % 2)) * ((k + 1) // 2)
        return (f // ring + dz) % depth * ring + (f % ring + dx) % ring

    barrier = pltpu.get_barrier_semaphore()

    def greet(slab_to, count):
        def one(i, carry):
            pl.semaphore_signal(
                barrier, inc=1, device_id=(slab_to, peer(i)), device_id_type=MESH
            )
            return carry

        lax.fori_loop(0, count, one, 0)

    greet(s, fronts - 1)

    @pl.when(s > 0)
    def _():
        greet(s - 1, fronts)

    @pl.when(s < last)
    def _():
        pl.semaphore_signal(barrier, inc=1, device_id=(s + 1, f), device_id_type=MESH)

    loads = []
    for h in range(halves):
        for c in range(2):
            at = (2 * h + c) * bnd
            loads.append(
                pltpu.make_async_copy(
                    inv_hbm.at[c, :, pl.ds(h * bnd, bnd)],
                    leaf2.at[:, pl.ds(at, bnd)],
                    load_sem.at[2 * h + c],
                )
            )
    for c in range(2):
        loads.append(
            pltpu.make_async_copy(
                cpl_hbm.at[c],
                cpl2.at[:, pl.ds(c * interior, interior)],
                load_sem.at[2 * halves + c],
            )
        )
    sep_loads = []
    for m in range(slots):
        for c in range(2):
            sep_loads.append(
                pltpu.make_async_copy(
                    sep_hbm.at[m, c],
                    sep2.at[m, :, pl.ds(c * sepw, sepw)],
                    sep_sem.at[2 * m + c],
                )
            )
    for copy in loads + sep_loads:
        copy.start()

    zero_block = jnp.zeros((2, rows, cols), BF16)
    rblk[pieces] = zero_block
    vals[positions] = zero_block
    run[cap] = jnp.zeros((2, rows, cols), F32)
    recv_b[cap] = zero_block
    recv_t[cap] = zero_block

    for h in range(halves):
        real = src_ref[0, pl.ds(h * bnd, bnd), :]
        imag = src_ref[1, pl.ds(h * bnd, bnd), :]
        top, low = pl.ds(2 * h * bnd, bnd), pl.ds((2 * h + 1) * bnd, bnd)
        xs[top, pl.ds(0, cols)] = real
        xs[top, pl.ds(cols, cols)] = imag
        xs[low, pl.ds(0, cols)] = -imag
        xs[low, pl.ds(cols, cols)] = real

    for copy in loads:
        copy.wait()
    base[...] = mm(leaf2[...], xs[...])
    rounded = base[...].astype(BF16)
    xb[pl.ds(0, interior), :] = rounded
    xb[pl.ds(interior, interior), pl.ds(0, cols)] = -rounded[:, cols:]
    xb[pl.ds(interior, interior), pl.ds(cols, cols)] = rounded[:, :cols]
    resid0[...] = mm(cpl2[...], xb[...])

    has_next = jnp.where(s < last, fronts, 0)
    has_prev = jnp.where(s > 0, 1, 0)
    pl.semaphore_wait(barrier, fronts - 1 + has_next + has_prev)

    def send_tag(i, carry):
        pltpu.make_async_remote_copy(
            src_ref=tab_ref,
            dst_ref=tag_recv.at[f],
            send_sem=tag_send,
            recv_sem=tag_arrive,
            device_id=(s, peer(i)),
            device_id_type=MESH,
        ).start()
        return carry

    lax.fori_loop(0, fronts - 1, send_tag, 0)
    tag_recv[f] = tab_ref[...]

    def prev_copy(slab_to):
        return pltpu.make_async_remote_copy(
            src_ref=tab_ref,
            dst_ref=tab_recv,
            send_sem=prev_send,
            recv_sem=prev_arrive,
            device_id=(slab_to, f),
            device_id_type=MESH,
        )

    def home_copy(slab_to):
        return pltpu.make_async_remote_copy(
            src_ref=inc,
            dst_ref=home,
            send_sem=home_send,
            recv_sem=home_arrive,
            device_id=(slab_to, f),
            device_id_type=MESH,
        )

    @pl.when(s < last)
    def _():
        prev_copy(s + 1).start()

    def await_bytes(buf, count, sem):
        view = buf.at[pl.ds(0, count)]
        pltpu.make_async_copy(view, view, sem).wait()

    def send_blocks(source, target, send_sem, recv_sem, slab_to, count):
        def one(i, carry):
            to = peer(i)
            pltpu.make_async_remote_copy(
                src_ref=source.at[pl.ds(2 * to, 2)],
                dst_ref=target.at[pl.ds(2 * f, 2)],
                send_sem=send_sem,
                recv_sem=recv_sem,
                device_id=(slab_to, to),
                device_id_type=MESH,
            ).start()
            return carry

        lax.fori_loop(0, count, one, 0)

    @pl.when(s == 0)
    def _():
        resid = resid0[...].astype(BF16)
        rblk[pl.ds(0, pieces), 0] = resid[:, :cols].reshape(pieces, rows, cols)
        rblk[pl.ds(0, pieces), 1] = resid[:, cols:].reshape(pieces, rows, cols)

    @pl.when(s > 0)
    def _():
        near = leaf2[:, pl.ds(0, 2 * bnd)]
        left = mm(cpl2[:, pl.ds(0, interior)], near)
        right = mm(cpl2[:, pl.ds(interior, interior)], near)
        comp2[:, pl.ds(0, bnd)] = (left[:, :bnd] - right[:, bnd:]).astype(BF16)
        comp2[:, pl.ds(bnd, bnd)] = (left[:, bnd:] + right[:, :bnd]).astype(BF16)
        prev_copy(s).wait_recv()
        bring = pltpu.make_async_copy(tab_recv, prev_smem, smem_sem)
        bring.start()
        bring.wait()
        await_bytes(recv_b, cap, b_arrive)
        for p in range(pieces):
            block = recv_b[prev_smem[2, p]]
            inc[p] = block
            at, low = pl.ds(p * rows, rows), pl.ds(bnd + p * rows, rows)
            xin[at, pl.ds(0, cols)] = block[0]
            xin[at, pl.ds(cols, cols)] = block[1]
            xin[low, pl.ds(0, cols)] = -block[1]
            xin[low, pl.ds(cols, cols)] = block[0]
        resid = (resid0[...] + mm(comp2[...], xin[...])).astype(BF16)
        rblk[pl.ds(0, pieces), 0] = resid[:, :cols].reshape(pieces, rows, cols)
        rblk[pl.ds(0, pieces), 1] = resid[:, cols:].reshape(pieces, rows, cols)

    for i in range(cap):
        out_a[i] = rblk[tab_smem[0, i]]
    send_blocks(out_a, recv_a, a_send, a_arrive, s, fronts - 1)
    for k in range(2):
        recv_a[2 * f + k] = out_a[2 * f + k]

    @pl.when(s > 0)
    def _():
        home_copy(s - 1).start()
        full = base[...] + mm(leaf2[:, pl.ds(0, 2 * bnd)], xin[...])
        sol_ref[0] = full[:, :cols].astype(BF16)
        sol_ref[1] = full[:, cols:].astype(BF16)

    @pl.when(s == 0)
    def _():
        sol_ref[0] = base[:, pl.ds(0, cols)].astype(BF16)
        sol_ref[1] = base[:, pl.ds(cols, cols)].astype(BF16)

    await_bytes(tag_recv, fronts - 1, tag_arrive)
    tags = tag_recv[:, 1, :]
    lane = lax.broadcasted_iota(jnp.int32, (fronts, LANES), 1)
    row = lax.broadcasted_iota(jnp.int32, (fronts, LANES), 0)
    first = jnp.sum(jnp.where(lane == 2 * f, tags, 0), axis=1, keepdims=True)
    second = jnp.sum(jnp.where(lane == 2 * f + 1, tags, 0), axis=1, keepdims=True)
    picked = jnp.where(lane % 2 == 0, first, second)
    back = jnp.sum(jnp.where(row == lane // 2, picked, 0), axis=0, keepdims=True)
    col = jnp.concatenate([first, second], axis=0)
    wide_lane = lax.broadcasted_iota(jnp.int32, (cap, LANES), 1)
    wide_row = lax.broadcasted_iota(jnp.int32, (cap, LANES), 0)
    as_row = jnp.sum(jnp.where(wide_lane == wide_row, col, 0), axis=0, keepdims=True)
    valid = wide_lane < cap
    same = valid & (as_row == col) & (wide_lane < wide_row)
    below = valid & (as_row < col)
    rank = jnp.sum(jnp.where(same | below, 1, 0), axis=1, keepdims=True)
    repeat = jnp.max(jnp.where(same, 1, 0), axis=1, keepdims=True)
    placed = rank == wide_lane
    where_at = wide_row % fronts * 2 + wide_row // fronts
    order = jnp.sum(jnp.where(placed, where_at, 0), axis=0, keepdims=True)
    keep = jnp.sum(jnp.where(placed, repeat, 0), axis=0, keepdims=True)
    upto = jnp.sum(jnp.where(col <= wide_lane, 1, 0), axis=0, keepdims=True)
    hit = jnp.max(jnp.where(col == wide_lane, 1, 0), axis=0, keepdims=True)
    ends = jnp.where(hit > 0, upto - 1, cap)
    own_tab[0:1, :] = order
    own_tab[1:2, :] = keep
    own_tab[2:3, :] = ends
    own_tab[3:4, :] = back
    own_tab[4:8, :] = jnp.zeros((4, LANES), jnp.int32)
    bring = pltpu.make_async_copy(own_tab, own_smem, smem_sem)
    bring.start()
    bring.wait()
    for copy in sep_loads:
        copy.wait()

    await_bytes(recv_a, cap - 2, a_arrive)
    total = jnp.zeros((2, rows, cols), F32)
    for i in range(cap):
        block = recv_a[own_smem[0, i]].astype(F32)
        total = jnp.where(own_smem[1, i] > 0, total, 0.0) + block
        run[i] = total
    for m in range(slots):
        for q in range(parts):
            block = run[own_smem[2, m * parts + q]].astype(BF16)
            at, low = pl.ds(q * rows, rows), pl.ds(sepw + q * rows, rows)
            xsep[m, at, pl.ds(0, cols)] = block[0]
            xsep[m, at, pl.ds(cols, cols)] = block[1]
            xsep[m, low, pl.ds(0, cols)] = -block[1]
            xsep[m, low, pl.ds(cols, cols)] = block[0]
    for m in range(slots):
        value = mm(sep2[m], xsep[m]).astype(BF16)
        at = pl.ds(m * parts, parts)
        vals[at, 0] = value[:, :cols].reshape(parts, rows, cols)
        vals[at, 1] = value[:, cols:].reshape(parts, rows, cols)
    for i in range(cap):
        out_b[i] = vals[own_smem[3, i]]

    @pl.when(s < last)
    def _():
        send_blocks(out_b, recv_b, b_send, b_arrive, s + 1, fronts)
        home_copy(s).wait_recv()
        trace_ref[...] = home[...]
        await_bytes(out_b, cap, b_send)
        prev_copy(s).wait_send()

    @pl.when(s == last)
    def _():
        send_blocks(out_b, recv_t, b_send, t_arrive, s, fronts - 1)
        for k in range(2):
            recv_t[2 * f + k] = out_b[2 * f + k]
        await_bytes(recv_t, cap - 2, t_arrive)
        for p in range(pieces):
            trace_ref[p] = recv_t[tab_smem[2, p]]
        await_bytes(out_b, cap - 2, b_send)

    @pl.when(s > 0)
    def _():
        home_copy(s).wait_send()

    await_bytes(out_a, cap - 2, a_send)
    await_bytes(tag_recv, fronts - 1, tag_send)


def tables(owners, count, targets, part_count, pieces, positions, fronts):
    sep_ids = jnp.arange(owners.shape[0], dtype=jnp.int32)
    earlier = (owners[:, None] == owners[None, :]) & (sep_ids[:, None] > sep_ids[None, :])
    slot_of = jnp.sum(jnp.where(earlier, 1, 0), axis=1).astype(jnp.int32)
    sep_of = targets // part_count
    match = sep_of[:, None] == sep_ids[None, :]
    destination = jnp.sum(jnp.where(match, owners[None, :], 0), axis=1)
    slot = jnp.sum(jnp.where(match, slot_of[None, :], 0), axis=1)
    position = slot * part_count + targets % part_count
    ids = jnp.arange(pieces, dtype=jnp.int32)
    usable = ids < count
    before = (
        (destination[:, None] == destination[None, :])
        & usable[None, :]
        & (ids[None, :] < ids[:, None])
    )
    rank = jnp.sum(jnp.where(before, 1, 0), axis=1).astype(jnp.int32)
    index = destination * 2 + rank
    lanes = jnp.arange(LANES, dtype=jnp.int32)
    route = (lanes[:, None] == index[None, :]) & usable[None, :]
    out_src = jnp.sum(jnp.where(route, ids[None, :] - pieces, 0), axis=1) + pieces
    tag = jnp.sum(jnp.where(route, position[None, :] - positions, 0), axis=1) + positions
    back = jnp.where(usable, index, 2 * fronts)
    back = jnp.pad(back, (0, LANES - pieces))
    blank = jnp.zeros((LANES,), jnp.int32)
    return jnp.stack([out_src, tag, back, blank, blank, blank, blank, blank]).astype(jnp.int32)


def solution(mesh):
    slabs, fronts = mesh.shape["slab"], mesh.shape["front"]
    ring = 4

    def body(source, leaf_inverse, boundary_map, sep_inverse, owner_map, piece_count, piece_target):
        src = source[0, 0]
        inv = leaf_inverse[0, 0]
        cpl = boundary_map[0, 0]
        sep = sep_inverse[0]
        interior, cols = src.shape[1], src.shape[2]
        bnd = cpl.shape[1]
        pieces = piece_target.shape[2]
        rows = bnd // pieces
        slots, sepw = sep.shape[0], sep.shape[2]
        parts = sepw // rows
        positions = slots * parts
        cap = 2 * fronts
        halves = interior // bnd
        tab = tables(
            owner_map[0], piece_count[0, 0], piece_target[0, 0], parts, pieces, positions, fronts
        )

        def blocks(count, dtype=BF16):
            return pltpu.VMEM((count, 2, rows, cols), dtype)

        vmem = pl.BlockSpec(memory_space=pltpu.VMEM)
        anyspace = pl.BlockSpec(memory_space=pl.ANY)
        smem = pl.BlockSpec(memory_space=pltpu.SMEM)
        dma = pltpu.SemaphoreType.DMA
        solved, trace = pl.pallas_call(
            functools.partial(sweep_kernel, slabs, fronts, ring),
            out_shape=(
                jax.ShapeDtypeStruct((2, interior, cols), BF16),
                jax.ShapeDtypeStruct((pieces, 2, rows, cols), BF16),
            ),
            in_specs=[vmem, anyspace, anyspace, anyspace, vmem, smem],
            out_specs=(vmem, vmem),
            scratch_shapes=[
                pltpu.VMEM((interior, 2 * interior), BF16),
                pltpu.VMEM((bnd, 2 * interior), BF16),
                pltpu.VMEM((slots, sepw, 2 * sepw), BF16),
                pltpu.VMEM((bnd, 2 * bnd), BF16),
                pltpu.VMEM((2 * interior, 2 * cols), BF16),
                pltpu.VMEM((2 * interior, 2 * cols), BF16),
                pltpu.VMEM((2 * bnd, 2 * cols), BF16),
                pltpu.VMEM((slots, 2 * sepw, 2 * cols), BF16),
                pltpu.VMEM((interior, 2 * cols), F32),
                pltpu.VMEM((bnd, 2 * cols), F32),
                blocks(pieces + 1),
                blocks(pieces),
                blocks(cap),
                blocks(cap),
                blocks(cap + 1, F32),
                blocks(positions + 1),
                blocks(cap),
                blocks(cap + 1),
                blocks(cap + 1),
                blocks(pieces),
                pltpu.VMEM((fronts, 8, LANES), jnp.int32),
                pltpu.VMEM((8, LANES), jnp.int32),
                pltpu.VMEM((8, LANES), jnp.int32),
                pltpu.SMEM((8, LANES), jnp.int32),
                pltpu.SMEM((8, LANES), jnp.int32),
                dma((2 * halves + 2,)),
                dma((2 * slots,)),
                dma,
                dma,
                dma,
                dma,
                dma,
                dma,
                dma,
                dma,
                dma,
                dma,
                dma,
                dma,
            ],
            compiler_params=pltpu.CompilerParams(
                collective_id=0, has_side_effects=True, vmem_limit_bytes=48 * 1024 * 1024
            ),
        )(src, inv, cpl, sep, tab, tab)
        return solved[None, None], trace[None, None]

    return jax.shard_map(
        body,
        mesh=mesh,
        in_specs=(
            P("slab", "front", None, None, None),
            P("slab", "front", None, None, None),
            P("slab", "front", None, None, None),
            P("slab", "front", None, None, None),
            P("slab", None),
            P("slab", "front"),
            P("slab", "front", None),
        ),
        out_specs=(
            P("slab", "front", None, None, None),
            P("slab", "front", None, None, None, None),
        ),
        check_vma=False,
    )
```

```python
import functools

import jax
import jax.numpy as jnp
from jax import lax
from jax.experimental import pallas as pl
from jax.experimental.pallas import tpu as pltpu
from jax.sharding import PartitionSpec as P

MESH = pl.DeviceIdType.MESH
BF16 = jnp.bfloat16
F32 = jnp.float32
I32 = jnp.int32
LANES = 128
HALF = LANES // 2
BATCHES = 2


def mm(a, b):
    return jnp.dot(a, b, preferred_element_type=F32)


def turn(x):
    return pltpu.roll(x, HALF, 1)


def iota(shape, axis):
    return lax.broadcasted_iota(I32, shape, axis)


def total(mask, value, axis):
    return jnp.sum(jnp.where(mask, value, 0), axis=axis, keepdims=True)


def as_column(row_value, size):
    shape = (size, size)
    return total(iota(shape, 0) == iota(shape, 1), row_value, 1)


def as_row(column, size):
    shape = (size, LANES)
    return total(iota(shape, 0) == iota(shape, 1), column, 0)


def leaf_tables(owners, targets, count, parts, positions, fronts):
    seps, pieces = owners.shape[1], targets.shape[1]
    square = (seps, seps)
    owner_col = as_column(owners, seps)
    slot_row = total((owner_col == owners) & (iota(square, 0) < iota(square, 1)), 1, 0)
    target_col = as_column(targets, pieces)
    wide = (pieces, seps)
    sep_id = iota(wide, 1)
    match = (target_col >= sep_id * parts) & (target_col < sep_id * parts + parts)
    destination = total(match, owners, 1)
    position = total(match, (slot_row - sep_id) * parts, 1) + target_col
    small = (pieces, pieces)
    piece_col, piece_row = iota(small, 0), iota(small, 1)
    destination_row = total(piece_col == piece_row, destination, 0)
    before = (destination == destination_row) & (piece_row < count) & (piece_row < piece_col)
    index = destination * 2 + total(before, 1, 1)
    shape = (pieces, LANES)
    piece_id, lane = iota(shape, 0), iota(shape, 1)
    usable = piece_id < count
    route = (lane == index) & usable
    out_src = total(route, piece_id - pieces, 0) + pieces
    tag = total(route, position - positions, 0) + positions
    back = total(piece_id == lane, jnp.where(usable, index, 2 * fronts), 0)
    return out_src, tag, back


def owner_tables(tags, f, fronts):
    cap = 2 * fronts
    lane, row = iota((fronts, LANES), 1), iota((fronts, LANES), 0)
    first = total(lane == 2 * f, tags, 1)
    second = total(lane == 2 * f + 1, tags, 1)
    picked = jnp.where(lane % 2 == 0, first, second)
    back = total(row == lane // 2, picked, 0)
    col = jnp.concatenate([first, second], axis=0)
    lane, row = iota((cap, LANES), 1), iota((cap, LANES), 0)
    tag_row = as_row(col, cap)
    valid = lane < cap
    same = valid & (tag_row == col) & (lane < row)
    rank = total(same | (valid & (tag_row < col)), 1, 1)
    repeat = jnp.max(jnp.where(same, 1, 0), axis=1, keepdims=True)
    placed = rank == lane
    order = total(placed, row % fronts * 2 + row // fronts, 0)
    keep = total(placed, repeat, 0)
    upto = total(col <= lane, 1, 0)
    hit = total(col == lane, 1, 0)
    ends = jnp.where(hit > 0, upto - 1, cap)
    return order, keep, ends, back


def sweep_kernel(
    slabs,
    fronts,
    ring,
    src_hbm,
    inv_hbm,
    cpl_hbm,
    sep_hbm,
    own_hbm,
    cnt_hbm,
    tgt_hbm,
    sol_ref,
    trace_ref,
    src_v,
    own_v,
    tgt_v,
    cnt_s,
    leaf2,
    cpl2,
    sep2,
    comp2,
    xs,
    xb,
    xin,
    xsep,
    base,
    resid0,
    rblk,
    inc,
    out_a,
    recv_a0,
    recv_a1,
    run,
    vals,
    out_b,
    recv_b0,
    recv_b1,
    recv_t,
    home,
    tag_v,
    tag_recv,
    leaf_tab,
    prev_tab,
    own_tab,
    leaf_smem,
    prev_smem,
    own_smem,
    small_sem,
    load_sem,
    sep_sem,
    tag_send,
    tag_arrive,
    prev_send,
    prev_arrive,
    a_send,
    a_arrive,
    b_send,
    b_arrive,
    t_arrive,
    home_send,
    home_arrive,
    smem_sem,
):
    s = lax.axis_index("slab")
    f = lax.axis_index("front")
    last = slabs - 1
    interior = src_v.shape[1]
    bnd = cpl2.shape[0]
    slots, sepw = sep2.shape[0], sep2.shape[1]
    pieces = inc.shape[0]
    rows = inc.shape[2]
    parts = sepw // rows
    positions = slots * parts
    cap = 2 * fronts
    halves = interior // bnd
    depth = fronts // ring
    recv_a, recv_b = (recv_a0, recv_a1), (recv_b0, recv_b1)
    lane_sets = [pl.ds(b * LANES, LANES) for b in range(BATCHES)]

    def peer(i):
        j, k = i // ring, i % ring
        dz = depth // 2 + (1 - 2 * (j % 2)) * ((j + 1) // 2)
        dx = ring // 2 + (1 - 2 * (k % 2)) * ((k + 1) // 2)
        return (f // ring + dz) % depth * ring + (f % ring + dx) % ring

    barrier = pltpu.get_barrier_semaphore()

    def greet(slab_to, count):
        def one(i, carry):
            pl.semaphore_signal(
                barrier, inc=1, device_id=(slab_to, peer(i)), device_id_type=MESH
            )
            return carry

        lax.fori_loop(0, count, one, 0)

    smalls = [
        pltpu.make_async_copy(own_hbm, own_v, small_sem.at[0]),
        pltpu.make_async_copy(tgt_hbm, tgt_v, small_sem.at[1]),
        pltpu.make_async_copy(cnt_hbm, cnt_s, small_sem.at[2]),
    ]
    load_src = pltpu.make_async_copy(src_hbm, src_v, small_sem.at[3])
    loads = []
    for h in range(halves):
        for c in range(2):
            at = (2 * h + c) * bnd
            loads.append(
                pltpu.make_async_copy(
                    inv_hbm.at[c, :, pl.ds(h * bnd, bnd)],
                    leaf2.at[:, pl.ds(at, bnd)],
                    load_sem.at[2 * h + c],
                )
            )
    cpl_loads = []
    for c in range(2):
        cpl_loads.append(
            pltpu.make_async_copy(
                cpl_hbm.at[c],
                cpl2.at[:, pl.ds(c * interior, interior)],
                load_sem.at[2 * halves + c],
            )
        )
    sep_loads = []
    for m in range(slots):
        for c in range(2):
            sep_loads.append(
                pltpu.make_async_copy(
                    sep_hbm.at[m, c],
                    sep2.at[m, :, pl.ds(c * sepw, sepw)],
                    sep_sem.at[2 * m + c],
                )
            )
    for copy in smalls + [load_src] + loads + cpl_loads:
        copy.start()

    @pl.when(s > 0)
    def _():
        greet(s - 1, fronts)

    greet(s, fronts - 1)

    @pl.when(s < last)
    def _():
        pl.semaphore_signal(barrier, inc=1, device_id=(s + 1, f), device_id_type=MESH)

    for copy in sep_loads:
        copy.start()

    zero_block = jnp.zeros((rows, LANES), BF16)
    run[cap] = jnp.zeros((rows, LANES), F32)
    for b in range(BATCHES):
        rblk[b, pieces] = zero_block
        vals[b, positions] = zero_block
        recv_b[b][cap] = zero_block
        recv_t[b, cap] = zero_block

    for copy in smalls:
        copy.wait()
    out_src, tag, back = leaf_tables(
        own_v[...], tgt_v[...], cnt_s[0, 0], parts, positions, fronts
    )
    leaf_tab[0:1, :] = out_src
    leaf_tab[1:2, :] = back
    leaf_tab[2:8, :] = jnp.zeros((6, LANES), I32)
    tag_v[...] = tag
    bring = pltpu.make_async_copy(leaf_tab, leaf_smem, smem_sem.at[0])
    bring.start()

    def low_half(like):
        return iota(like.shape, 1) < HALF

    def swap(x):
        turned = turn(x)
        return jnp.where(low_half(x), -turned, turned)

    load_src.wait()
    for h in range(halves):
        real = src_v[0, pl.ds(h * bnd, bnd), :]
        imag = src_v[1, pl.ds(h * bnd, bnd), :]
        top, low = pl.ds(2 * h * bnd, bnd), pl.ds((2 * h + 1) * bnd, bnd)
        packed = (
            jnp.where(low_half(real), real, turn(imag)),
            jnp.where(low_half(real), turn(real), imag),
        )
        for b in range(BATCHES):
            xs[top, lane_sets[b]] = packed[b]
            xs[low, lane_sets[b]] = swap(packed[b])

    for copy in loads:
        copy.wait()
    base[...] = mm(leaf2[...], xs[...])
    for b in range(BATCHES):
        rounded = base[:, lane_sets[b]].astype(BF16)
        xb[pl.ds(0, interior), lane_sets[b]] = rounded
        xb[pl.ds(interior, interior), lane_sets[b]] = swap(rounded)
    for copy in cpl_loads:
        copy.wait()
    resid0[...] = mm(cpl2[...], xb[...])
    bring.wait()

    has_next = jnp.where(s < last, fronts, 0)
    has_prev = jnp.where(s > 0, 1, 0)
    pl.semaphore_wait(barrier, fronts - 1 + has_next + has_prev)

    def push_tag(to):
        pltpu.make_async_remote_copy(
            src_ref=tag_v,
            dst_ref=tag_recv.at[f],
            send_sem=tag_send,
            recv_sem=tag_arrive,
            device_id=(s, to),
            device_id_type=MESH,
        ).start()

    def send_blocks(source, target, send_sem, recv_sem, slab_to, count, tagged=False):
        def one(i, carry):
            to = peer(i)
            if tagged:
                push_tag(to)
            pltpu.make_async_remote_copy(
                src_ref=source.at[pl.ds(2 * to, 2)],
                dst_ref=target.at[pl.ds(2 * f, 2)],
                send_sem=send_sem,
                recv_sem=recv_sem,
                device_id=(slab_to, to),
                device_id_type=MESH,
            ).start()
            return carry

        lax.fori_loop(0, count, one, 0)

    def prev_copy(slab_to):
        return pltpu.make_async_remote_copy(
            src_ref=leaf_tab,
            dst_ref=prev_tab,
            send_sem=prev_send,
            recv_sem=prev_arrive,
            device_id=(slab_to, f),
            device_id_type=MESH,
        )

    def home_copy(slab_to):
        return pltpu.make_async_remote_copy(
            src_ref=inc,
            dst_ref=home,
            send_sem=home_send,
            recv_sem=home_arrive,
            device_id=(slab_to, f),
            device_id_type=MESH,
        )

    def await_bytes(buf, count, sem):
        view = buf.at[pl.ds(0, count)]
        pltpu.make_async_copy(view, view, sem).wait()

    def push_resid(b, resid, tagged):
        rblk[b, pl.ds(0, pieces)] = resid.astype(BF16).reshape(pieces, rows, LANES)
        for i in range(cap):
            out_a[b, i] = rblk[b, leaf_smem[0, i]]
        send_blocks(
            out_a.at[b], recv_a[b], a_send.at[b], a_arrive.at[b], s, fronts - 1, tagged
        )
        for k in range(2):
            recv_a[b][2 * f + k] = out_a[b, 2 * f + k]

    def make_owner_tables():
        await_bytes(tag_recv, fronts - 1, tag_arrive)
        order, keep, ends, ret = owner_tables(tag_recv[:, 0, :], f, fronts)
        own_tab[0:1, :] = order
        own_tab[1:2, :] = keep
        own_tab[2:3, :] = ends
        own_tab[3:4, :] = ret
        own_tab[4:8, :] = jnp.zeros((4, LANES), I32)
        bring = pltpu.make_async_copy(own_tab, own_smem, smem_sem.at[1])
        bring.start()
        bring.wait()

    def unpack(b0, b1):
        first = low_half(b0)
        return jnp.where(first, b0, turn(b1)), jnp.where(first, turn(b0), b1)

    tag_recv[f] = tag_v[...]

    @pl.when(s == 0)
    def _():
        for b in range(BATCHES):
            push_resid(b, resid0[:, lane_sets[b]], b == 0)
        prev_copy(s + 1).start()
        real, imag = unpack(base[:, lane_sets[0]], base[:, lane_sets[1]])
        sol_ref[0] = real.astype(BF16)
        sol_ref[1] = imag.astype(BF16)
        make_owner_tables()

    @pl.when(s > 0)
    def _():
        def one(i, carry):
            push_tag(peer(i))
            return carry

        lax.fori_loop(0, fronts - 1, one, 0)

        @pl.when(s < last)
        def _():
            prev_copy(s + 1).start()

        near = leaf2[:, pl.ds(0, 2 * bnd)]
        left = mm(cpl2[:, pl.ds(0, interior)], near)
        right = mm(cpl2[:, pl.ds(interior, interior)], near)
        comp2[:, pl.ds(0, bnd)] = (left[:, :bnd] - right[:, bnd:]).astype(BF16)
        comp2[:, pl.ds(bnd, bnd)] = (left[:, bnd:] + right[:, :bnd]).astype(BF16)
        prev_copy(s).wait_recv()
        bring = pltpu.make_async_copy(prev_tab, prev_smem, smem_sem.at[0])
        bring.start()
        bring.wait()
        make_owner_tables()
        for b in range(BATCHES):
            await_bytes(recv_b[b], cap, b_arrive.at[b])
            for p in range(pieces):
                block = recv_b[b][prev_smem[1, p]]
                xin[pl.ds(p * rows, rows), lane_sets[b]] = block
                xin[pl.ds(bnd + p * rows, rows), lane_sets[b]] = swap(block)
            push_resid(b, resid0[:, lane_sets[b]] + mm(comp2[...], xin[:, lane_sets[b]]), False)
        for p in range(pieces):
            at = pl.ds(p * rows, rows)
            real, imag = unpack(xin[at, lane_sets[0]], xin[at, lane_sets[1]])
            inc[p, 0] = real
            inc[p, 1] = imag
        home_copy(s - 1).start()
        full = base[...] + mm(leaf2[:, pl.ds(0, 2 * bnd)], xin[...])
        real, imag = unpack(full[:, :LANES], full[:, LANES:])
        sol_ref[0] = real.astype(BF16)
        sol_ref[1] = imag.astype(BF16)

    for copy in sep_loads:
        copy.wait()

    for b in range(BATCHES):
        await_bytes(recv_a[b], cap - 2, a_arrive.at[b])
        running = jnp.zeros((rows, LANES), F32)
        for i in range(cap):
            block = recv_a[b][own_smem[0, i]].astype(F32)
            running = jnp.where(own_smem[1, i] > 0, running, 0.0) + block
            run[i] = running
        for m in range(slots):
            for q in range(parts):
                block = run[own_smem[2, m * parts + q]].astype(BF16)
                xsep[m, pl.ds(q * rows, rows), :] = block
                xsep[m, pl.ds(sepw + q * rows, rows), :] = swap(block)
        for m in range(slots):
            value = mm(sep2[m], xsep[m]).astype(BF16)
            vals[b, pl.ds(m * parts, parts)] = value.reshape(parts, rows, LANES)
        for i in range(cap):
            out_b[b, i] = vals[b, own_smem[3, i]]

        @pl.when(s < last)
        def _():
            send_blocks(
                out_b.at[b], recv_b[b], b_send.at[b], b_arrive.at[b], s + 1, fronts
            )

        @pl.when(s == last)
        def _():
            send_blocks(
                out_b.at[b], recv_t.at[b], b_send.at[b], t_arrive.at[b], s, fronts - 1
            )
            for k in range(2):
                recv_t[b, 2 * f + k] = out_b[b, 2 * f + k]

    @pl.when(s < last)
    def _():
        home_copy(s).wait_recv()
        trace_ref[...] = home[...]
        for b in range(BATCHES):
            await_bytes(out_b.at[b], cap, b_send.at[b])
        prev_copy(s).wait_send()

    @pl.when(s == last)
    def _():
        for b in range(BATCHES):
            await_bytes(recv_t.at[b], cap - 2, t_arrive.at[b])
        for p in range(pieces):
            at = leaf_smem[1, p]
            real, imag = unpack(recv_t[0, at], recv_t[1, at])
            trace_ref[p, 0] = real
            trace_ref[p, 1] = imag
        for b in range(BATCHES):
            await_bytes(out_b.at[b], cap - 2, b_send.at[b])

    @pl.when(s > 0)
    def _():
        home_copy(s).wait_send()

    for b in range(BATCHES):
        await_bytes(out_a.at[b], cap - 2, a_send.at[b])
    await_bytes(tag_recv, fronts - 1, tag_send)


def solution(mesh):
    slabs, fronts = mesh.shape["slab"], mesh.shape["front"]
    ring = 4

    def body(source, leaf_inverse, boundary_map, sep_inverse, owner_map, piece_count, piece_target):
        src = source[0, 0]
        inv = leaf_inverse[0, 0]
        cpl = boundary_map[0, 0]
        sep = sep_inverse[0]
        interior, cols = src.shape[1], src.shape[2]
        bnd = cpl.shape[1]
        seps, pieces = owner_map.shape[1], piece_target.shape[2]
        rows = bnd // pieces
        slots, sepw = sep.shape[0], sep.shape[2]
        positions = slots * (sepw // rows)
        cap = 2 * fronts
        halves = interior // bnd

        def blocks(count):
            return pltpu.VMEM((BATCHES, count, rows, LANES), BF16)

        def single(count):
            return pltpu.VMEM((count, rows, LANES), BF16)

        vmem = pl.BlockSpec(memory_space=pltpu.VMEM)
        anyspace = pl.BlockSpec(memory_space=pl.ANY)
        dma = pltpu.SemaphoreType.DMA
        table = pltpu.VMEM((8, LANES), I32)
        smem_table = pltpu.SMEM((8, LANES), I32)
        solved, trace = pl.pallas_call(
            functools.partial(sweep_kernel, slabs, fronts, ring),
            out_shape=(
                jax.ShapeDtypeStruct((2, interior, cols), BF16),
                jax.ShapeDtypeStruct((pieces, 2, rows, cols), BF16),
            ),
            in_specs=[anyspace] * 7,
            out_specs=(vmem, vmem),
            scratch_shapes=[
                pltpu.VMEM((2, interior, cols), BF16),
                pltpu.VMEM((1, seps), I32),
                pltpu.VMEM((1, pieces), I32),
                pltpu.SMEM((1, 1), I32),
                pltpu.VMEM((interior, 2 * interior), BF16),
                pltpu.VMEM((bnd, 2 * interior), BF16),
                pltpu.VMEM((slots, sepw, 2 * sepw), BF16),
                pltpu.VMEM((bnd, 2 * bnd), BF16),
                pltpu.VMEM((2 * interior, 2 * cols), BF16),
                pltpu.VMEM((2 * interior, 2 * cols), BF16),
                pltpu.VMEM((2 * bnd, 2 * cols), BF16),
                pltpu.VMEM((slots, 2 * sepw, LANES), BF16),
                pltpu.VMEM((interior, 2 * cols), F32),
                pltpu.VMEM((bnd, 2 * cols), F32),
                blocks(pieces + 1),
                pltpu.VMEM((pieces, 2, rows, cols), BF16),
                blocks(cap),
                single(cap),
                single(cap),
                pltpu.VMEM((cap + 1, rows, LANES), F32),
                blocks(positions + 1),
                blocks(cap),
                single(cap + 1),
                single(cap + 1),
                blocks(cap + 1),
                pltpu.VMEM((pieces, 2, rows, cols), BF16),
                pltpu.VMEM((1, LANES), I32),
                pltpu.VMEM((fronts, 1, LANES), I32),
                table,
                table,
                table,
                smem_table,
                smem_table,
                smem_table,
                dma((4,)),
                dma((2 * halves + 2,)),
                dma((2 * slots,)),
                dma,
                dma,
                dma,
                dma,
                dma((BATCHES,)),
                dma((BATCHES,)),
                dma((BATCHES,)),
                dma((BATCHES,)),
                dma((BATCHES,)),
                dma,
                dma,
                dma((2,)),
            ],
            compiler_params=pltpu.CompilerParams(
                collective_id=0, has_side_effects=True, vmem_limit_bytes=60 * 1024 * 1024
            ),
        )(src, inv, cpl, sep, owner_map, piece_count, piece_target[0])
        return solved[None, None], trace[None, None]

    return jax.shard_map(
        body,
        mesh=mesh,
        in_specs=(
            P("slab", "front", None, None, None),
            P("slab", "front", None, None, None),
            P("slab", "front", None, None, None),
            P("slab", "front", None, None, None),
            P("slab", None),
            P("slab", "front"),
            P("slab", "front", None),
        ),
        out_specs=(
            P("slab", "front", None, None, None),
            P("slab", "front", None, None, None, None),
        ),
        check_vma=False,
    )
```

```python
import functools

import jax
import jax.numpy as jnp
from jax import lax
from jax.experimental import pallas as pl
from jax.experimental.pallas import tpu as pltpu
from jax.sharding import PartitionSpec as P

MESH = pl.DeviceIdType.MESH
BF16 = jnp.bfloat16
F32 = jnp.float32
I32 = jnp.int32
LANES = 128
HALF = LANES // 2
BATCHES = 2


def mm(a, b):
    return jnp.dot(a, b, preferred_element_type=F32)


def turn(x):
    return pltpu.roll(x, HALF, 1)


def iota(shape, axis):
    return lax.broadcasted_iota(I32, shape, axis)


def total(mask, value, axis):
    return jnp.sum(jnp.where(mask, value, 0), axis=axis, keepdims=True)


def as_column(row_value, size):
    shape = (size, size)
    return total(iota(shape, 0) == iota(shape, 1), row_value, 1)


def as_row(column, size):
    shape = (size, LANES)
    return total(iota(shape, 0) == iota(shape, 1), column, 0)


def leaf_tables(owners, targets, count, parts, positions, fronts):
    seps, pieces = owners.shape[1], targets.shape[1]
    square = (seps, seps)
    owner_col = as_column(owners, seps)
    slot_row = total((owner_col == owners) & (iota(square, 0) < iota(square, 1)), 1, 0)
    target_col = as_column(targets, pieces)
    wide = (pieces, seps)
    sep_id = iota(wide, 1)
    match = (target_col >= sep_id * parts) & (target_col < sep_id * parts + parts)
    destination = total(match, owners, 1)
    position = total(match, (slot_row - sep_id) * parts, 1) + target_col
    small = (pieces, pieces)
    piece_col, piece_row = iota(small, 0), iota(small, 1)
    destination_row = total(piece_col == piece_row, destination, 0)
    before = (destination == destination_row) & (piece_row < count) & (piece_row < piece_col)
    index = destination * 2 + total(before, 1, 1)
    shape = (pieces, LANES)
    piece_id, lane = iota(shape, 0), iota(shape, 1)
    usable = piece_id < count
    route = (lane == index) & usable
    out_src = total(route, piece_id - pieces, 0) + pieces
    tag = total(route, position - positions, 0) + positions
    back = total(piece_id == lane, jnp.where(usable, index, 2 * fronts), 0)
    return out_src, tag, back


def owner_tables(tags, f, fronts):
    cap = 2 * fronts
    lane, row = iota((fronts, LANES), 1), iota((fronts, LANES), 0)
    first = total(lane == 2 * f, tags, 1)
    second = total(lane == 2 * f + 1, tags, 1)
    picked = jnp.where(lane % 2 == 0, first, second)
    back = total(row == lane // 2, picked, 0)
    col = jnp.concatenate([first, second], axis=0)
    lane, row = iota((cap, LANES), 1), iota((cap, LANES), 0)
    tag_row = as_row(col, cap)
    valid = lane < cap
    same = valid & (tag_row == col) & (lane < row)
    rank = total(same | (valid & (tag_row < col)), 1, 1)
    repeat = jnp.max(jnp.where(same, 1, 0), axis=1, keepdims=True)
    placed = rank == lane
    order = total(placed, row % fronts * 2 + row // fronts, 0)
    keep = total(placed, repeat, 0)
    upto = total(col <= lane, 1, 0)
    hit = total(col == lane, 1, 0)
    ends = jnp.where(hit > 0, upto - 1, cap)
    return order, keep, ends, back


def stay(x):
    return pltpu.with_memory_space_constraint(x, pltpu.HBM)


def around(size):
    half = size // 2
    return [half + (1 - 2 * (j % 2)) * ((j + 1) // 2) for j in range(size)]


def ordered_offsets(depth, ring):
    offsets = [(dz, dx) for dx in around(ring) for dz in around(depth)]
    return sorted(offsets, key=lambda o: -min(o[0], depth - o[0]) - min(o[1], ring - o[1]))


def sweep_kernel(
    slabs,
    fronts,
    ring,
    src_hbm,
    inv_hbm,
    cpl_hbm,
    sep_hbm,
    own_hbm,
    cnt_hbm,
    tgt_hbm,
    sol_ref,
    trace_ref,
    src_v,
    own_v,
    tgt_v,
    cnt_s,
    leaf2,
    cpl2,
    sep2,
    comp2,
    xs,
    xb,
    xin,
    xsep,
    base,
    resid0,
    rblk,
    inc,
    out_a,
    recv_a0,
    recv_a1,
    run,
    vals,
    out_b,
    recv_b0,
    recv_b1,
    recv_t,
    home,
    tag_v,
    tag_recv,
    leaf_tab,
    prev_tab,
    own_tab,
    leaf_smem,
    prev_smem,
    own_smem,
    small_sem,
    load_sem,
    sep_sem,
    tag_send,
    tag_arrive,
    prev_send,
    prev_arrive,
    a_send,
    a_arrive,
    b_send,
    b_arrive,
    t_arrive,
    home_send,
    home_arrive,
    smem_sem,
):
    s = lax.axis_index("slab")
    f = lax.axis_index("front")
    last = slabs - 1
    interior = src_v.shape[1]
    bnd = cpl2.shape[0]
    slots, sepw = sep2.shape[0], sep2.shape[1]
    pieces = inc.shape[0]
    rows = inc.shape[2]
    parts = sepw // rows
    positions = slots * parts
    cap = 2 * fronts
    halves = interior // bnd
    depth = fronts // ring
    recv_a, recv_b = (recv_a0, recv_a1), (recv_b0, recv_b1)
    lane_sets = [pl.ds(b * LANES, LANES) for b in range(BATCHES)]

    f_z, f_x = lax.div(f, ring), lax.rem(f, ring)
    z_of = [lax.rem(f_z + dz, depth) * ring for dz in range(depth)]
    x_of = [lax.rem(f_x + dx, ring) for dx in range(ring)]

    def peers(count):
        for dz, dx in ordered_offsets(depth, ring)[:count]:
            yield z_of[dz] + x_of[dx]

    barrier = pltpu.get_barrier_semaphore()

    def greet(slab_to, count):
        for to in peers(count):
            pl.semaphore_signal(barrier, inc=1, device_id=(slab_to, to), device_id_type=MESH)

    smalls = [
        pltpu.make_async_copy(own_hbm, own_v, small_sem.at[0]),
        pltpu.make_async_copy(tgt_hbm, tgt_v, small_sem.at[1]),
        pltpu.make_async_copy(cnt_hbm, cnt_s, small_sem.at[2]),
    ]
    load_src = pltpu.make_async_copy(src_hbm, src_v, small_sem.at[3])
    loads = []
    for h in range(halves):
        for c in range(2):
            at = (2 * h + c) * bnd
            loads.append(
                pltpu.make_async_copy(
                    inv_hbm.at[c, :, pl.ds(h * bnd, bnd)],
                    leaf2.at[:, pl.ds(at, bnd)],
                    load_sem.at[2 * h + c],
                )
            )
    cpl_loads = []
    for c in range(2):
        cpl_loads.append(
            pltpu.make_async_copy(
                cpl_hbm.at[c],
                cpl2.at[:, pl.ds(c * interior, interior)],
                load_sem.at[2 * halves + c],
            )
        )
    sep_loads = []
    for m in range(slots):
        for c in range(2):
            sep_loads.append(
                pltpu.make_async_copy(
                    sep_hbm.at[m, c],
                    sep2.at[m, :, pl.ds(c * sepw, sepw)],
                    sep_sem.at[2 * m + c],
                )
            )
    for copy in smalls + [load_src] + loads + cpl_loads:
        copy.start()

    @pl.when(s > 0)
    def _():
        greet(s - 1, fronts)

    greet(s, fronts - 1)

    @pl.when(s < last)
    def _():
        pl.semaphore_signal(barrier, inc=1, device_id=(s + 1, f), device_id_type=MESH)

    for copy in sep_loads:
        copy.start()

    zero_block = jnp.zeros((rows, LANES), BF16)
    run[cap] = jnp.zeros((rows, LANES), F32)
    for b in range(BATCHES):
        rblk[b, pieces] = zero_block
        vals[b, positions] = zero_block
        recv_b[b][cap] = zero_block
        recv_t[b, cap] = zero_block

    for copy in smalls:
        copy.wait()
    out_src, tag, back = leaf_tables(
        own_v[...], tgt_v[...], cnt_s[0, 0], parts, positions, fronts
    )
    leaf_tab[0:1, :] = out_src
    leaf_tab[1:2, :] = back
    leaf_tab[2:8, :] = jnp.zeros((6, LANES), I32)
    tag_v[...] = tag
    bring = pltpu.make_async_copy(leaf_tab, leaf_smem, smem_sem.at[0])
    bring.start()

    def low_half(like):
        return iota(like.shape, 1) < HALF

    def swap(x):
        turned = turn(x)
        return jnp.where(low_half(x), -turned, turned)

    load_src.wait()
    for h in range(halves):
        real = src_v[0, pl.ds(h * bnd, bnd), :]
        imag = src_v[1, pl.ds(h * bnd, bnd), :]
        top, low = pl.ds(2 * h * bnd, bnd), pl.ds((2 * h + 1) * bnd, bnd)
        packed = (
            jnp.where(low_half(real), real, turn(imag)),
            jnp.where(low_half(real), turn(real), imag),
        )
        for b in range(BATCHES):
            xs[top, lane_sets[b]] = packed[b]
            xs[low, lane_sets[b]] = swap(packed[b])

    for copy in loads:
        copy.wait()
    base[...] = mm(leaf2[...], xs[...])
    for b in range(BATCHES):
        rounded = base[:, lane_sets[b]].astype(BF16)
        xb[pl.ds(0, interior), lane_sets[b]] = rounded
        xb[pl.ds(interior, interior), lane_sets[b]] = swap(rounded)
    for copy in cpl_loads:
        copy.wait()
    resid0[...] = mm(cpl2[...], xb[...])
    bring.wait()

    has_next = jnp.where(s < last, fronts, 0)
    has_prev = jnp.where(s > 0, 1, 0)
    pl.semaphore_wait(barrier, fronts - 1 + has_next + has_prev)

    def push_tags():
        for to in peers(fronts - 1):
            pltpu.make_async_remote_copy(
                src_ref=tag_v,
                dst_ref=tag_recv.at[f],
                send_sem=tag_send,
                recv_sem=tag_arrive,
                device_id=(s, to),
                device_id_type=MESH,
            ).start()

    def send_blocks(source, target, send_sem, recv_sem, slab_to, count):
        for to in peers(count):
            pltpu.make_async_remote_copy(
                src_ref=source.at[pl.ds(2 * to, 2)],
                dst_ref=target.at[pl.ds(2 * f, 2)],
                send_sem=send_sem,
                recv_sem=recv_sem,
                device_id=(slab_to, to),
                device_id_type=MESH,
            ).start()

    def prev_copy(slab_to):
        return pltpu.make_async_remote_copy(
            src_ref=leaf_tab,
            dst_ref=prev_tab,
            send_sem=prev_send,
            recv_sem=prev_arrive,
            device_id=(slab_to, f),
            device_id_type=MESH,
        )

    def home_copy(slab_to):
        return pltpu.make_async_remote_copy(
            src_ref=inc,
            dst_ref=home,
            send_sem=home_send,
            recv_sem=home_arrive,
            device_id=(slab_to, f),
            device_id_type=MESH,
        )

    def await_bytes(buf, count, sem):
        view = buf.at[pl.ds(0, count)]
        pltpu.make_async_copy(view, view, sem).wait()

    def put_resid(b, resid):
        rblk[b, pl.ds(0, pieces)] = resid.astype(BF16).reshape(pieces, rows, LANES)

    def push_resid(b):
        for i in range(cap):
            out_a[b, i] = rblk[b, leaf_smem[0, i]]
        send_blocks(out_a.at[b], recv_a[b], a_send.at[b], a_arrive.at[b], s, fronts - 1)
        for k in range(2):
            recv_a[b][2 * f + k] = out_a[b, 2 * f + k]

    def make_owner_tables():
        await_bytes(tag_recv, fronts - 1, tag_arrive)
        order, keep, ends, ret = owner_tables(tag_recv[:, 0, :], f, fronts)
        own_tab[0:1, :] = order
        own_tab[1:2, :] = keep
        own_tab[2:3, :] = ends
        own_tab[3:4, :] = ret
        own_tab[4:8, :] = jnp.zeros((4, LANES), I32)
        bring = pltpu.make_async_copy(own_tab, own_smem, smem_sem.at[1])
        bring.start()
        bring.wait()

    def unpack(b0, b1):
        first = low_half(b0)
        return jnp.where(first, b0, turn(b1)), jnp.where(first, turn(b0), b1)

    tag_recv[f] = tag_v[...]

    @pl.when(s > 0)
    def _():
        push_tags()

        @pl.when(s < last)
        def _():
            prev_copy(s + 1).start()

        near = leaf2[:, pl.ds(0, 2 * bnd)]
        left = mm(cpl2[:, pl.ds(0, interior)], near)
        right = mm(cpl2[:, pl.ds(interior, interior)], near)
        comp2[:, pl.ds(0, bnd)] = (left[:, :bnd] - right[:, bnd:]).astype(BF16)
        comp2[:, pl.ds(bnd, bnd)] = (left[:, bnd:] + right[:, :bnd]).astype(BF16)
        prev_copy(s).wait_recv()
        bring = pltpu.make_async_copy(prev_tab, prev_smem, smem_sem.at[0])
        bring.start()
        bring.wait()
        make_owner_tables()

    for b in range(BATCHES):

        @pl.when(s > 0)
        def _():
            await_bytes(recv_b[b], cap, b_arrive.at[b])
            for p in range(pieces):
                block = recv_b[b][prev_smem[1, p]]
                xin[pl.ds(p * rows, rows), lane_sets[b]] = block
                xin[pl.ds(bnd + p * rows, rows), lane_sets[b]] = swap(block)
            put_resid(b, resid0[:, lane_sets[b]] + mm(comp2[...], xin[:, lane_sets[b]]))

        @pl.when(s == 0)
        def _():
            put_resid(b, resid0[:, lane_sets[b]])

        push_resid(b)
        if b == 0:

            @pl.when(s == 0)
            def _():
                push_tags()

    @pl.when(s == 0)
    def _():
        prev_copy(s + 1).start()
        real, imag = unpack(base[:, lane_sets[0]], base[:, lane_sets[1]])
        sol_ref[0] = real.astype(BF16)
        sol_ref[1] = imag.astype(BF16)
        make_owner_tables()

    @pl.when(s > 0)
    def _():
        for p in range(pieces):
            at = pl.ds(p * rows, rows)
            real, imag = unpack(xin[at, lane_sets[0]], xin[at, lane_sets[1]])
            inc[p, 0] = real
            inc[p, 1] = imag
        home_copy(s - 1).start()
        full = base[...] + mm(leaf2[:, pl.ds(0, 2 * bnd)], xin[...])
        real, imag = unpack(full[:, :LANES], full[:, LANES:])
        sol_ref[0] = real.astype(BF16)
        sol_ref[1] = imag.astype(BF16)

    for copy in sep_loads:
        copy.wait()

    for b in range(BATCHES):
        await_bytes(recv_a[b], cap - 2, a_arrive.at[b])
        running = jnp.zeros((rows, LANES), F32)
        for i in range(cap):
            block = recv_a[b][own_smem[0, i]].astype(F32)
            running = jnp.where(own_smem[1, i] > 0, running, 0.0) + block
            run[i] = running
        for m in range(slots):
            for q in range(parts):
                block = run[own_smem[2, m * parts + q]].astype(BF16)
                xsep[m, pl.ds(q * rows, rows), :] = block
                xsep[m, pl.ds(sepw + q * rows, rows), :] = swap(block)
        for m in range(slots):
            value = mm(sep2[m], xsep[m]).astype(BF16)
            vals[b, pl.ds(m * parts, parts)] = value.reshape(parts, rows, LANES)
        for i in range(cap):
            out_b[b, i] = vals[b, own_smem[3, i]]

        @pl.when(s < last)
        def _():
            send_blocks(
                out_b.at[b], recv_b[b], b_send.at[b], b_arrive.at[b], s + 1, fronts
            )

        @pl.when(s == last)
        def _():
            send_blocks(
                out_b.at[b], recv_t.at[b], b_send.at[b], t_arrive.at[b], s, fronts - 1
            )
            for k in range(2):
                recv_t[b, 2 * f + k] = out_b[b, 2 * f + k]

    @pl.when(s < last)
    def _():
        home_copy(s).wait_recv()
        trace_ref[...] = home[...]
        for b in range(BATCHES):
            await_bytes(out_b.at[b], cap, b_send.at[b])
        prev_copy(s).wait_send()

    @pl.when(s == last)
    def _():
        for b in range(BATCHES):
            await_bytes(recv_t.at[b], cap - 2, t_arrive.at[b])
        for p in range(pieces):
            at = leaf_smem[1, p]
            real, imag = unpack(recv_t[0, at], recv_t[1, at])
            trace_ref[p, 0] = real
            trace_ref[p, 1] = imag
        for b in range(BATCHES):
            await_bytes(out_b.at[b], cap - 2, b_send.at[b])

    @pl.when(s > 0)
    def _():
        home_copy(s).wait_send()

    for b in range(BATCHES):
        await_bytes(out_a.at[b], cap - 2, a_send.at[b])
    await_bytes(tag_recv, fronts - 1, tag_send)


def solution(mesh):
    slabs, fronts = mesh.shape["slab"], mesh.shape["front"]
    ring = 4

    def body(source, leaf_inverse, boundary_map, sep_inverse, owner_map, piece_count, piece_target):
        src = source[0, 0]
        inv = leaf_inverse[0, 0]
        cpl = boundary_map[0, 0]
        sep = sep_inverse[0]
        interior, cols = src.shape[1], src.shape[2]
        bnd = cpl.shape[1]
        seps, pieces = owner_map.shape[1], piece_target.shape[2]
        rows = bnd // pieces
        slots, sepw = sep.shape[0], sep.shape[2]
        positions = slots * (sepw // rows)
        cap = 2 * fronts
        halves = interior // bnd

        def blocks(count):
            return pltpu.VMEM((BATCHES, count, rows, LANES), BF16)

        def single(count):
            return pltpu.VMEM((count, rows, LANES), BF16)

        vmem = pl.BlockSpec(memory_space=pltpu.VMEM)
        anyspace = pl.BlockSpec(memory_space=pltpu.HBM)
        dma = pltpu.SemaphoreType.DMA
        table = pltpu.VMEM((8, LANES), I32)
        smem_table = pltpu.SMEM((8, LANES), I32)
        solved, trace = pl.pallas_call(
            functools.partial(sweep_kernel, slabs, fronts, ring),
            out_shape=(
                jax.ShapeDtypeStruct((2, interior, cols), BF16),
                jax.ShapeDtypeStruct((pieces, 2, rows, cols), BF16),
            ),
            in_specs=[anyspace] * 5 + [pl.BlockSpec(memory_space=pl.ANY), anyspace],
            out_specs=(vmem, vmem),
            scratch_shapes=[
                pltpu.VMEM((2, interior, cols), BF16),
                pltpu.VMEM((1, seps), I32),
                pltpu.VMEM((1, pieces), I32),
                pltpu.SMEM((1, 1), I32),
                pltpu.VMEM((interior, 2 * interior), BF16),
                pltpu.VMEM((bnd, 2 * interior), BF16),
                pltpu.VMEM((slots, sepw, 2 * sepw), BF16),
                pltpu.VMEM((bnd, 2 * bnd), BF16),
                pltpu.VMEM((2 * interior, 2 * cols), BF16),
                pltpu.VMEM((2 * interior, 2 * cols), BF16),
                pltpu.VMEM((2 * bnd, 2 * cols), BF16),
                pltpu.VMEM((slots, 2 * sepw, LANES), BF16),
                pltpu.VMEM((interior, 2 * cols), F32),
                pltpu.VMEM((bnd, 2 * cols), F32),
                blocks(pieces + 1),
                pltpu.VMEM((pieces, 2, rows, cols), BF16),
                blocks(cap),
                single(cap),
                single(cap),
                pltpu.VMEM((cap + 1, rows, LANES), F32),
                blocks(positions + 1),
                blocks(cap),
                single(cap + 1),
                single(cap + 1),
                blocks(cap + 1),
                pltpu.VMEM((pieces, 2, rows, cols), BF16),
                pltpu.VMEM((1, LANES), I32),
                pltpu.VMEM((fronts, 1, LANES), I32),
                table,
                table,
                table,
                smem_table,
                smem_table,
                smem_table,
                dma((4,)),
                dma((2 * halves + 2,)),
                dma((2 * slots,)),
                dma,
                dma,
                dma,
                dma,
                dma((BATCHES,)),
                dma((BATCHES,)),
                dma((BATCHES,)),
                dma((BATCHES,)),
                dma((BATCHES,)),
                dma,
                dma,
                dma((2,)),
            ],
            compiler_params=pltpu.CompilerParams(
                collective_id=0, has_side_effects=True, vmem_limit_bytes=40 * 1024 * 1024
            ),
        )(stay(src), stay(inv), stay(cpl), stay(sep), stay(owner_map), piece_count, stay(piece_target[0]))
        return solved[None, None], trace[None, None]

    return jax.shard_map(
        body,
        mesh=mesh,
        in_specs=(
            P("slab", "front", None, None, None),
            P("slab", "front", None, None, None),
            P("slab", "front", None, None, None),
            P("slab", "front", None, None, None),
            P("slab", None),
            P("slab", "front"),
            P("slab", "front", None),
        ),
        out_specs=(
            P("slab", "front", None, None, None),
            P("slab", "front", None, None, None, None),
        ),
        check_vma=False,
    )
```

```python
import functools

import jax
import jax.numpy as jnp
from jax import lax
from jax.experimental import pallas as pl
from jax.experimental.pallas import tpu as pltpu
from jax.sharding import PartitionSpec as P

MESH = pl.DeviceIdType.MESH
BF16 = jnp.bfloat16
F32 = jnp.float32
I32 = jnp.int32
LANES = 128
HALF = LANES // 2
QUARTER = LANES // 4
BATCHES = 4
GROUPS = 2


def mm(a, b):
    return jnp.dot(a, b, preferred_element_type=F32)


def turn(x, distance=HALF):
    return pltpu.roll(x, distance, 1)


def iota(shape, axis):
    return lax.broadcasted_iota(I32, shape, axis)


def low_half(x):
    return iota(x.shape, len(x.shape) - 1) < HALF


def quarters(a, b, c, d):
    lane = iota(a.shape, 1)
    front = jnp.where(lane < QUARTER, a, b)
    return jnp.where(lane < HALF, front, jnp.where(lane < HALF + QUARTER, c, d))


def group_swap(x):
    left, right = turn(x, LANES - QUARTER), turn(x, QUARTER)
    return quarters(-left, right, -left, right)


def twin_swap(x):
    moved = turn(x, QUARTER)
    return quarters(-moved, moved, -moved, moved)


def twins(x):
    turned, low = turn(x), low_half(x)
    return jnp.where(low, x, turned), jnp.where(low, turned, x)


def split_groups(real, imag):
    left, right = LANES - QUARTER, QUARTER
    return (
        quarters(real, turn(imag, right), turn(real, right), turn(imag)),
        quarters(turn(real), turn(imag, left), turn(real, left), imag),
    )


def join_groups(g0, g1):
    left, right = LANES - QUARTER, QUARTER
    g0_left, g1_right = turn(g0, left), turn(g1, right)
    return (
        quarters(g0, g0_left, turn(g1), g1_right),
        quarters(g0_left, turn(g0), g1_right, g1),
    )


def total(mask, value, axis):
    return jnp.sum(jnp.where(mask, value, 0), axis=axis, keepdims=True)


def as_column(row_value, size):
    shape = (size, size)
    return total(iota(shape, 0) == iota(shape, 1), row_value, 1)


def as_row(column, size):
    shape = (size, LANES)
    return total(iota(shape, 0) == iota(shape, 1), column, 0)


def leaf_tables(owners, targets, count, parts, positions, fronts):
    seps, pieces = owners.shape[1], targets.shape[1]
    square = (seps, seps)
    owner_col = as_column(owners, seps)
    slot_row = total((owner_col == owners) & (iota(square, 0) < iota(square, 1)), 1, 0)
    target_col = as_column(targets, pieces)
    wide = (pieces, seps)
    sep_id = iota(wide, 1)
    match = (target_col >= sep_id * parts) & (target_col < sep_id * parts + parts)
    destination = total(match, owners, 1)
    position = total(match, (slot_row - sep_id) * parts, 1) + target_col
    small = (pieces, pieces)
    piece_col, piece_row = iota(small, 0), iota(small, 1)
    destination_row = total(piece_col == piece_row, destination, 0)
    before = (destination == destination_row) & (piece_row < count) & (piece_row < piece_col)
    index = destination * 2 + total(before, 1, 1)
    shape = (pieces, LANES)
    piece_id, lane = iota(shape, 0), iota(shape, 1)
    usable = piece_id < count
    route = (lane == index) & usable
    out_src = total(route, piece_id - pieces, 0) + pieces
    tag = total(route, position - positions, 0) + positions
    back = total(piece_id == lane, jnp.where(usable, index, 2 * fronts), 0)
    return out_src, tag, back


def owner_tables(tags, f, fronts):
    cap = 2 * fronts
    lane, row = iota((fronts, LANES), 1), iota((fronts, LANES), 0)
    first = total(lane == 2 * f, tags, 1)
    second = total(lane == 2 * f + 1, tags, 1)
    picked = jnp.where(lane % 2 == 0, first, second)
    back = total(row == lane // 2, picked, 0)
    col = jnp.concatenate([first, second], axis=0)
    lane, row = iota((cap, LANES), 1), iota((cap, LANES), 0)
    tag_row = as_row(col, cap)
    valid = lane < cap
    same = valid & (tag_row == col) & (lane < row)
    rank = total(same | (valid & (tag_row < col)), 1, 1)
    repeat = jnp.max(jnp.where(same, 1, 0), axis=1, keepdims=True)
    placed = rank == lane
    order = total(placed, row % fronts * 2 + row // fronts, 0)
    keep = total(placed, repeat, 0)
    upto = total(col <= lane, 1, 0)
    hit = total(col == lane, 1, 0)
    ends = jnp.where(hit > 0, upto - 1, cap)
    return order, keep, ends, back


def stay(x):
    return pltpu.with_memory_space_constraint(x, pltpu.HBM)


def around(size):
    half = size // 2
    return [half + (1 - 2 * (j % 2)) * ((j + 1) // 2) for j in range(size)]


def ordered_offsets(depth, ring):
    offsets = [(dz, dx) for dx in around(ring) for dz in around(depth)]
    return sorted(offsets, key=lambda o: -min(o[0], depth - o[0]) - min(o[1], ring - o[1]))


def sweep_kernel(
    slabs,
    fronts,
    ring,
    src_hbm,
    inv_hbm,
    cpl_hbm,
    sep_hbm,
    own_hbm,
    cnt_hbm,
    tgt_hbm,
    sol_ref,
    trace_ref,
    src_v,
    own_v,
    tgt_v,
    cnt_s,
    leaf2,
    cpl2,
    sep2,
    comp2,
    xs,
    xb,
    xin,
    xtwin,
    xsep,
    base,
    resid0,
    rblk,
    inc,
    out_a,
    recv_a0,
    recv_a1,
    recv_a2,
    recv_a3,
    run,
    vals,
    out_b,
    recv_b0,
    recv_b1,
    recv_b2,
    recv_b3,
    recv_t,
    home,
    tag_v,
    tag_recv,
    leaf_tab,
    prev_tab,
    own_tab,
    leaf_smem,
    prev_smem,
    own_smem,
    small_sem,
    load_sem,
    sep_sem,
    tag_send,
    tag_arrive,
    prev_send,
    prev_arrive,
    a_send,
    a_arrive,
    b_send,
    b_arrive,
    t_arrive,
    home_send,
    home_arrive,
    smem_sem,
):
    s = lax.axis_index("slab")
    f = lax.axis_index("front")
    last = slabs - 1
    interior = src_v.shape[1]
    bnd = cpl2.shape[0]
    slots, sepw = sep2.shape[0], sep2.shape[1]
    pieces = inc.shape[0]
    rows = inc.shape[2]
    thin = rows // 2
    parts = sepw // rows
    positions = slots * parts
    cap = 2 * fronts
    halves = interior // bnd
    depth = fronts // ring
    recv_a = (recv_a0, recv_a1, recv_a2, recv_a3)
    recv_b = (recv_b0, recv_b1, recv_b2, recv_b3)
    lane_sets = [pl.ds(b * LANES, LANES) for b in range(GROUPS)]

    f_z, f_x = lax.div(f, ring), lax.rem(f, ring)
    z_of = [lax.rem(f_z + dz, depth) * ring for dz in range(depth)]
    x_of = [lax.rem(f_x + dx, ring) for dx in range(ring)]

    def peers(count):
        for dz, dx in ordered_offsets(depth, ring)[:count]:
            yield z_of[dz] + x_of[dx]

    barrier = pltpu.get_barrier_semaphore()

    def greet(slab_to, count):
        for to in peers(count):
            pl.semaphore_signal(barrier, inc=1, device_id=(slab_to, to), device_id_type=MESH)

    smalls = [
        pltpu.make_async_copy(own_hbm, own_v, small_sem.at[0]),
        pltpu.make_async_copy(tgt_hbm, tgt_v, small_sem.at[1]),
        pltpu.make_async_copy(cnt_hbm, cnt_s, small_sem.at[2]),
    ]
    load_src = pltpu.make_async_copy(src_hbm, src_v, small_sem.at[3])
    loads = []
    for h in range(halves):
        for c in range(2):
            at = (2 * h + c) * bnd
            loads.append(
                pltpu.make_async_copy(
                    inv_hbm.at[c, :, pl.ds(h * bnd, bnd)],
                    leaf2.at[:, pl.ds(at, bnd)],
                    load_sem.at[2 * h + c],
                )
            )
    cpl_loads = []
    for c in range(2):
        cpl_loads.append(
            pltpu.make_async_copy(
                cpl_hbm.at[c],
                cpl2.at[:, pl.ds(c * interior, interior)],
                load_sem.at[2 * halves + c],
            )
        )
    sep_loads = []
    for m in range(slots):
        for c in range(2):
            sep_loads.append(
                pltpu.make_async_copy(
                    sep_hbm.at[m, c],
                    sep2.at[m, :, pl.ds(c * sepw, sepw)],
                    sep_sem.at[2 * m + c],
                )
            )
    for copy in smalls + [load_src] + loads + cpl_loads:
        copy.start()

    @pl.when(s > 0)
    def _():
        greet(s - 1, fronts)

    greet(s, fronts - 1)

    @pl.when(s < last)
    def _():
        pl.semaphore_signal(barrier, inc=1, device_id=(s + 1, f), device_id_type=MESH)

    for copy in sep_loads:
        copy.start()

    zero_block = jnp.zeros((thin, LANES), BF16)
    run[cap] = jnp.zeros((thin, LANES), F32)
    for b in range(BATCHES):
        rblk[b, pieces] = zero_block
        vals[b, positions] = zero_block
        recv_b[b][cap] = zero_block
        recv_t[b, cap] = zero_block

    for copy in smalls:
        copy.wait()
    out_src, tag, back = leaf_tables(
        own_v[...], tgt_v[...], cnt_s[0, 0], parts, positions, fronts
    )
    leaf_tab[0:1, :] = out_src
    leaf_tab[1:2, :] = back
    leaf_tab[2:8, :] = jnp.zeros((6, LANES), I32)
    tag_v[...] = tag
    bring = pltpu.make_async_copy(leaf_tab, leaf_smem, smem_sem.at[0])
    bring.start()

    load_src.wait()
    for h in range(halves):
        real = src_v[0, pl.ds(h * bnd, bnd), :]
        imag = src_v[1, pl.ds(h * bnd, bnd), :]
        top, low = pl.ds(2 * h * bnd, bnd), pl.ds((2 * h + 1) * bnd, bnd)
        packed = split_groups(real, imag)
        for g in range(GROUPS):
            xs[top, lane_sets[g]] = packed[g]
            xs[low, lane_sets[g]] = group_swap(packed[g])

    for copy in loads:
        copy.wait()
    base[...] = mm(leaf2[...], xs[...])
    for g in range(GROUPS):
        rounded = base[:, lane_sets[g]].astype(BF16)
        xb[pl.ds(0, interior), lane_sets[g]] = rounded
        xb[pl.ds(interior, interior), lane_sets[g]] = group_swap(rounded)
    for copy in cpl_loads:
        copy.wait()
    start_resid = mm(cpl2[...], xb[...])
    for g in range(GROUPS):
        pair = twins(start_resid[:, g * LANES : (g + 1) * LANES])
        resid0[2 * g], resid0[2 * g + 1] = pair
    bring.wait()

    has_next = jnp.where(s < last, fronts, 0)
    has_prev = jnp.where(s > 0, 1, 0)
    pl.semaphore_wait(barrier, fronts - 1 + has_next + has_prev)

    def push_tags():
        for to in peers(fronts - 1):
            pltpu.make_async_remote_copy(
                src_ref=tag_v,
                dst_ref=tag_recv.at[f],
                send_sem=tag_send,
                recv_sem=tag_arrive,
                device_id=(s, to),
                device_id_type=MESH,
            ).start()

    def send_blocks(source, target, send_sem, recv_sem, slab_to, count):
        for to in peers(count):
            pltpu.make_async_remote_copy(
                src_ref=source.at[pl.ds(2 * to, 2)],
                dst_ref=target.at[pl.ds(2 * f, 2)],
                send_sem=send_sem,
                recv_sem=recv_sem,
                device_id=(slab_to, to),
                device_id_type=MESH,
            ).start()

    def prev_copy(slab_to):
        return pltpu.make_async_remote_copy(
            src_ref=leaf_tab,
            dst_ref=prev_tab,
            send_sem=prev_send,
            recv_sem=prev_arrive,
            device_id=(slab_to, f),
            device_id_type=MESH,
        )

    def home_copy(slab_to):
        return pltpu.make_async_remote_copy(
            src_ref=inc,
            dst_ref=home,
            send_sem=home_send,
            recv_sem=home_arrive,
            device_id=(slab_to, f),
            device_id_type=MESH,
        )

    def await_bytes(buf, count, sem):
        view = buf.at[pl.ds(0, count)]
        pltpu.make_async_copy(view, view, sem).wait()

    def pack(value, count):
        block = value.astype(BF16).reshape(count, rows, LANES)
        upper, lower = block[:, :thin], block[:, thin:]
        return jnp.where(low_half(upper), upper, lower)

    def spread(block, put):
        for k, part in enumerate(twins(block)):
            put(0, k * thin, part)
            put(1, k * thin, twin_swap(part))

    def put_resid(b, resid):
        rblk[b, pl.ds(0, pieces)] = pack(resid, pieces)

    def push_resid(b):
        for i in range(cap):
            out_a[b, i] = rblk[b, leaf_smem[0, i]]
        send_blocks(out_a.at[b], recv_a[b], a_send.at[b], a_arrive.at[b], s, fronts - 1)
        for k in range(2):
            recv_a[b][2 * f + k] = out_a[b, 2 * f + k]

    def make_owner_tables():
        await_bytes(tag_recv, fronts - 1, tag_arrive)
        order, keep, ends, ret = owner_tables(tag_recv[:, 0, :], f, fronts)
        own_tab[0:1, :] = order
        own_tab[1:2, :] = keep
        own_tab[2:3, :] = ends
        own_tab[3:4, :] = ret
        own_tab[4:8, :] = jnp.zeros((4, LANES), I32)
        bring = pltpu.make_async_copy(own_tab, own_smem, smem_sem.at[1])
        bring.start()
        bring.wait()

    tag_recv[f] = tag_v[...]

    @pl.when(s > 0)
    def _():
        push_tags()

        @pl.when(s < last)
        def _():
            prev_copy(s + 1).start()

        near = leaf2[:, pl.ds(0, 2 * bnd)]
        left = mm(cpl2[:, pl.ds(0, interior)], near)
        right = mm(cpl2[:, pl.ds(interior, interior)], near)
        comp2[:, pl.ds(0, bnd)] = (left[:, :bnd] - right[:, bnd:]).astype(BF16)
        comp2[:, pl.ds(bnd, bnd)] = (left[:, bnd:] + right[:, :bnd]).astype(BF16)
        prev_copy(s).wait_recv()
        bring = pltpu.make_async_copy(prev_tab, prev_smem, smem_sem.at[0])
        bring.start()
        bring.wait()
        make_owner_tables()

    for b in range(BATCHES):

        @pl.when(s > 0)
        def _():
            await_bytes(recv_b[b], cap, b_arrive.at[b])
            for p in range(pieces):

                def put(which, offset, part):
                    xtwin[b, pl.ds(which * bnd + p * rows + offset, thin), :] = part

                spread(recv_b[b][prev_smem[1, p]], put)
            put_resid(b, resid0[b] + mm(comp2[...], xtwin[b]))

        @pl.when(s == 0)
        def _():
            put_resid(b, resid0[b])

        push_resid(b)
        if b == 0:

            @pl.when(s == 0)
            def _():
                push_tags()

    @pl.when(s == 0)
    def _():
        prev_copy(s + 1).start()
        make_owner_tables()

    @pl.when(s > 0)
    def _():
        for g in range(GROUPS):
            even, odd = xtwin[2 * g], xtwin[2 * g + 1]
            xin[:, lane_sets[g]] = jnp.where(low_half(even), even, odd)
        real, imag = join_groups(xin[pl.ds(0, bnd), lane_sets[0]], xin[pl.ds(0, bnd), lane_sets[1]])
        inc[:, 0] = real.reshape(pieces, rows, LANES)
        inc[:, 1] = imag.reshape(pieces, rows, LANES)
        home_copy(s - 1).start()

    def put_solution(full):
        full = full.astype(BF16)
        sol_ref[0], sol_ref[1] = join_groups(full[:, :LANES], full[:, LANES:])

    for copy in sep_loads:
        copy.wait()

    for b in range(BATCHES):
        await_bytes(recv_a[b], cap - 2, a_arrive.at[b])
        running = jnp.zeros((thin, LANES), F32)
        for i in range(cap):
            block = recv_a[b][own_smem[0, i]].astype(F32)
            running = jnp.where(own_smem[1, i] > 0, running, 0.0) + block
            run[i] = running
        for m in range(slots):
            for q in range(parts):

                def put(which, offset, part):
                    xsep[m, pl.ds(which * sepw + q * rows + offset, thin), :] = part

                spread(run[own_smem[2, m * parts + q]].astype(BF16), put)
        for m in range(slots):
            vals[b, pl.ds(m * parts, parts)] = pack(mm(sep2[m], xsep[m]), parts)
        for i in range(cap):
            out_b[b, i] = vals[b, own_smem[3, i]]

        @pl.when(s < last)
        def _():
            send_blocks(
                out_b.at[b], recv_b[b], b_send.at[b], b_arrive.at[b], s + 1, fronts
            )

        @pl.when(s == last)
        def _():
            send_blocks(
                out_b.at[b], recv_t.at[b], b_send.at[b], t_arrive.at[b], s, fronts - 1
            )
            for k in range(2):
                recv_t[b, 2 * f + k] = out_b[b, 2 * f + k]

    @pl.when(s == 0)
    def _():
        put_solution(base[...])

    @pl.when(s > 0)
    def _():
        put_solution(base[...] + mm(leaf2[:, pl.ds(0, 2 * bnd)], xin[...]))

    @pl.when(s < last)
    def _():
        home_copy(s).wait_recv()
        trace_ref[...] = home[...]
        for b in range(BATCHES):
            await_bytes(out_b.at[b], cap, b_send.at[b])
        prev_copy(s).wait_send()

    @pl.when(s == last)
    def _():
        for b in range(BATCHES):
            await_bytes(recv_t.at[b], cap - 2, t_arrive.at[b])
        for p in range(pieces):
            at = leaf_smem[1, p]
            pairs = [twins(recv_t[b, at]) for b in range(BATCHES)]
            for k in range(2):
                low = low_half(pairs[0][k])
                real, imag = join_groups(
                    jnp.where(low, pairs[0][k], pairs[1][k]),
                    jnp.where(low, pairs[2][k], pairs[3][k]),
                )
                trace_ref[p, 0, pl.ds(k * thin, thin), :] = real
                trace_ref[p, 1, pl.ds(k * thin, thin), :] = imag
        for b in range(BATCHES):
            await_bytes(out_b.at[b], cap - 2, b_send.at[b])

    @pl.when(s > 0)
    def _():
        home_copy(s).wait_send()

    for b in range(BATCHES):
        await_bytes(out_a.at[b], cap - 2, a_send.at[b])
    await_bytes(tag_recv, fronts - 1, tag_send)


def solution(mesh):
    slabs, fronts = mesh.shape["slab"], mesh.shape["front"]
    ring = 4

    def body(source, leaf_inverse, boundary_map, sep_inverse, owner_map, piece_count, piece_target):
        src = source[0, 0]
        inv = leaf_inverse[0, 0]
        cpl = boundary_map[0, 0]
        sep = sep_inverse[0]
        interior, cols = src.shape[1], src.shape[2]
        bnd = cpl.shape[1]
        seps, pieces = owner_map.shape[1], piece_target.shape[2]
        rows = bnd // pieces
        slots, sepw = sep.shape[0], sep.shape[2]
        positions = slots * (sepw // rows)
        cap = 2 * fronts
        halves = interior // bnd

        def blocks(count):
            return pltpu.VMEM((BATCHES, count, rows // 2, LANES), BF16)

        def single(count):
            return pltpu.VMEM((count, rows // 2, LANES), BF16)

        vmem = pl.BlockSpec(memory_space=pltpu.VMEM)
        anyspace = pl.BlockSpec(memory_space=pltpu.HBM)
        dma = pltpu.SemaphoreType.DMA
        table = pltpu.VMEM((8, LANES), I32)
        smem_table = pltpu.SMEM((8, LANES), I32)
        solved, trace = pl.pallas_call(
            functools.partial(sweep_kernel, slabs, fronts, ring),
            out_shape=(
                jax.ShapeDtypeStruct((2, interior, cols), BF16),
                jax.ShapeDtypeStruct((pieces, 2, rows, cols), BF16),
            ),
            in_specs=[anyspace] * 5 + [pl.BlockSpec(memory_space=pl.ANY), anyspace],
            out_specs=(vmem, vmem),
            scratch_shapes=[
                pltpu.VMEM((2, interior, cols), BF16),
                pltpu.VMEM((1, seps), I32),
                pltpu.VMEM((1, pieces), I32),
                pltpu.SMEM((1, 1), I32),
                pltpu.VMEM((interior, 2 * interior), BF16),
                pltpu.VMEM((bnd, 2 * interior), BF16),
                pltpu.VMEM((slots, sepw, 2 * sepw), BF16),
                pltpu.VMEM((bnd, 2 * bnd), BF16),
                pltpu.VMEM((2 * interior, 2 * cols), BF16),
                pltpu.VMEM((2 * interior, 2 * cols), BF16),
                pltpu.VMEM((2 * bnd, 2 * cols), BF16),
                pltpu.VMEM((BATCHES, 2 * bnd, LANES), BF16),
                pltpu.VMEM((slots, 2 * sepw, LANES), BF16),
                pltpu.VMEM((interior, 2 * cols), F32),
                pltpu.VMEM((BATCHES, bnd, LANES), F32),
                blocks(pieces + 1),
                pltpu.VMEM((pieces, 2, rows, cols), BF16),
                blocks(cap),
                single(cap),
                single(cap),
                single(cap),
                single(cap),
                pltpu.VMEM((cap + 1, rows // 2, LANES), F32),
                blocks(positions + 1),
                blocks(cap),
                single(cap + 1),
                single(cap + 1),
                single(cap + 1),
                single(cap + 1),
                blocks(cap + 1),
                pltpu.VMEM((pieces, 2, rows, cols), BF16),
                pltpu.VMEM((1, LANES), I32),
                pltpu.VMEM((fronts, 1, LANES), I32),
                table,
                table,
                table,
                smem_table,
                smem_table,
                smem_table,
                dma((4,)),
                dma((2 * halves + 2,)),
                dma((2 * slots,)),
                dma,
                dma,
                dma,
                dma,
                dma((BATCHES,)),
                dma((BATCHES,)),
                dma((BATCHES,)),
                dma((BATCHES,)),
                dma((BATCHES,)),
                dma,
                dma,
                dma((2,)),
            ],
            compiler_params=pltpu.CompilerParams(
                collective_id=0, has_side_effects=True, vmem_limit_bytes=40 * 1024 * 1024
            ),
        )(stay(src), stay(inv), stay(cpl), stay(sep), stay(owner_map), piece_count, stay(piece_target[0]))
        return solved[None, None], trace[None, None]

    return jax.shard_map(
        body,
        mesh=mesh,
        in_specs=(
            P("slab", "front", None, None, None),
            P("slab", "front", None, None, None),
            P("slab", "front", None, None, None),
            P("slab", "front", None, None, None),
            P("slab", None),
            P("slab", "front"),
            P("slab", "front", None),
        ),
        out_specs=(
            P("slab", "front", None, None, None),
            P("slab", "front", None, None, None, None),
        ),
        check_vma=False,
    )
```

```python
import functools

import jax
import jax.numpy as jnp
from jax import lax
from jax.experimental import pallas as pl
from jax.experimental.pallas import tpu as pltpu
from jax.sharding import PartitionSpec as P

MESH = pl.DeviceIdType.MESH
BF16 = jnp.bfloat16
F32 = jnp.float32
I32 = jnp.int32
LANES = 128
HALF = LANES // 2
QUARTER = LANES // 4
BATCHES = 4
GROUPS = 2


def mm(a, b):
    return jnp.dot(a, b, preferred_element_type=F32)


def turn(x, distance=HALF):
    return pltpu.roll(x, distance, 1)


def iota(shape, axis):
    return lax.broadcasted_iota(I32, shape, axis)


def low_half(x):
    return iota(x.shape, len(x.shape) - 1) < HALF


def quarters(a, b, c, d):
    lane = iota(a.shape, 1)
    front = jnp.where(lane < QUARTER, a, b)
    return jnp.where(lane < HALF, front, jnp.where(lane < HALF + QUARTER, c, d))


def group_swap(x):
    left, right = turn(x, LANES - QUARTER), turn(x, QUARTER)
    return quarters(-left, right, -left, right)


def twin_swap(x):
    moved = turn(x, QUARTER)
    return quarters(-moved, moved, -moved, moved)


def twins(x):
    turned, low = turn(x), low_half(x)
    return jnp.where(low, x, turned), jnp.where(low, turned, x)


def split_groups(real, imag):
    left, right = LANES - QUARTER, QUARTER
    return (
        quarters(real, turn(imag, right), turn(real, right), turn(imag)),
        quarters(turn(real), turn(imag, left), turn(real, left), imag),
    )


def join_groups(g0, g1):
    left, right = LANES - QUARTER, QUARTER
    g0_left, g1_right = turn(g0, left), turn(g1, right)
    return (
        quarters(g0, g0_left, turn(g1), g1_right),
        quarters(g0_left, turn(g0), g1_right, g1),
    )


def total(mask, value, axis):
    return jnp.sum(jnp.where(mask, value, 0), axis=axis, keepdims=True)


def as_column(row_value, size):
    shape = (size, size)
    return total(iota(shape, 0) == iota(shape, 1), row_value, 1)


def as_row(column, size):
    shape = (size, LANES)
    return total(iota(shape, 0) == iota(shape, 1), column, 0)


def leaf_tables(owners, targets, count, parts, positions, fronts):
    seps, pieces = owners.shape[1], targets.shape[1]
    square = (seps, seps)
    owner_col = as_column(owners, seps)
    slot_row = total((owner_col == owners) & (iota(square, 0) < iota(square, 1)), 1, 0)
    target_col = as_column(targets, pieces)
    wide = (pieces, seps)
    sep_id = iota(wide, 1)
    match = (target_col >= sep_id * parts) & (target_col < sep_id * parts + parts)
    destination = total(match, owners, 1)
    position = total(match, (slot_row - sep_id) * parts, 1) + target_col
    small = (pieces, pieces)
    piece_col, piece_row = iota(small, 0), iota(small, 1)
    destination_row = total(piece_col == piece_row, destination, 0)
    before = (destination == destination_row) & (piece_row < count) & (piece_row < piece_col)
    index = destination * 2 + total(before, 1, 1)
    shape = (pieces, LANES)
    piece_id, lane = iota(shape, 0), iota(shape, 1)
    usable = piece_id < count
    route = (lane == index) & usable
    out_src = total(route, piece_id - pieces, 0) + pieces
    tag = total(route, position - positions, 0) + positions
    back = total(piece_id == lane, jnp.where(usable, index, 2 * fronts), 0)
    return out_src, tag, back


def owner_tables(tags, f, fronts):
    cap = 2 * fronts
    lane, row = iota((fronts, LANES), 1), iota((fronts, LANES), 0)
    first = total(lane == 2 * f, tags, 1)
    second = total(lane == 2 * f + 1, tags, 1)
    picked = jnp.where(lane % 2 == 0, first, second)
    back = total(row == lane // 2, picked, 0)
    col = jnp.concatenate([first, second], axis=0)
    lane, row = iota((cap, LANES), 1), iota((cap, LANES), 0)
    tag_row = as_row(col, cap)
    valid = lane < cap
    same = valid & (tag_row == col) & (lane < row)
    rank = total(same | (valid & (tag_row < col)), 1, 1)
    repeat = jnp.max(jnp.where(same, 1, 0), axis=1, keepdims=True)
    placed = rank == lane
    order = total(placed, row % fronts * 2 + row // fronts, 0)
    keep = total(placed, repeat, 0)
    upto = total(col <= lane, 1, 0)
    hit = total(col == lane, 1, 0)
    ends = jnp.where(hit > 0, upto - 1, cap)
    return order, keep, ends, back


def stay(x):
    return pltpu.with_memory_space_constraint(x, pltpu.HBM)


def around(size):
    half = size // 2
    return [half + (1 - 2 * (j % 2)) * ((j + 1) // 2) for j in range(size)]


def ordered_offsets(depth, ring):
    offsets = [(dz, dx) for dx in around(ring) for dz in around(depth)]
    return sorted(offsets, key=lambda o: -min(o[0], depth - o[0]) - min(o[1], ring - o[1]))


def sweep_kernel(
    slabs,
    fronts,
    ring,
    src_hbm,
    inv_hbm,
    cpl_hbm,
    sep_hbm,
    own_hbm,
    cnt_hbm,
    tgt_hbm,
    sol_ref,
    trace_ref,
    src_v,
    own_v,
    tgt_v,
    cnt_s,
    leaf2,
    cpl2,
    sep2,
    comp2,
    xs,
    xb,
    xin,
    xtwin,
    xsep,
    base,
    resid0,
    rblk,
    inc,
    out_a,
    recv_a0,
    recv_a1,
    recv_a2,
    recv_a3,
    run,
    vals,
    out_b,
    recv_b0,
    recv_b1,
    recv_b2,
    recv_b3,
    recv_t,
    home,
    tag_v,
    tag_recv,
    leaf_tab,
    prev_tab,
    own_tab,
    leaf_smem,
    prev_smem,
    own_smem,
    small_sem,
    load_sem,
    sep_sem,
    tag_send,
    tag_arrive,
    prev_send,
    prev_arrive,
    a_send,
    a_arrive,
    b_send,
    b_arrive,
    t_arrive,
    home_send,
    home_arrive,
    smem_sem,
):
    s = lax.axis_index("slab")
    f = lax.axis_index("front")
    last = slabs - 1
    interior = src_v.shape[1]
    bnd = cpl2.shape[0]
    slots, sepw = sep2.shape[0], sep2.shape[1]
    pieces = inc.shape[0]
    rows = inc.shape[2]
    thin = rows // 2
    parts = sepw // rows
    positions = slots * parts
    cap = 2 * fronts
    halves = interior // bnd
    depth = fronts // ring
    recv_a = (recv_a0, recv_a1, recv_a2, recv_a3)
    recv_b = (recv_b0, recv_b1, recv_b2, recv_b3)
    lane_sets = [pl.ds(b * LANES, LANES) for b in range(GROUPS)]

    f_z, f_x = lax.div(f, ring), lax.rem(f, ring)
    z_of = [lax.rem(f_z + dz, depth) * ring for dz in range(depth)]
    x_of = [lax.rem(f_x + dx, ring) for dx in range(ring)]

    def peers(count):
        for dz, dx in ordered_offsets(depth, ring)[:count]:
            yield z_of[dz] + x_of[dx]

    barrier = pltpu.get_barrier_semaphore()

    def greet(slab_to, count):
        for to in peers(count):
            pl.semaphore_signal(barrier, inc=1, device_id=(slab_to, to), device_id_type=MESH)

    smalls = [
        pltpu.make_async_copy(own_hbm, own_v, small_sem.at[0]),
        pltpu.make_async_copy(tgt_hbm, tgt_v, small_sem.at[1]),
        pltpu.make_async_copy(cnt_hbm, cnt_s, small_sem.at[2]),
    ]
    load_src = pltpu.make_async_copy(src_hbm, src_v, small_sem.at[3])
    loads = []
    for h in range(halves):
        for c in range(2):
            at = (2 * h + c) * bnd
            loads.append(
                pltpu.make_async_copy(
                    inv_hbm.at[c, :, pl.ds(h * bnd, bnd)],
                    leaf2.at[:, pl.ds(at, bnd)],
                    load_sem.at[2 * h + c],
                )
            )
    cpl_loads = []
    for c in range(2):
        cpl_loads.append(
            pltpu.make_async_copy(
                cpl_hbm.at[c],
                cpl2.at[:, pl.ds(c * interior, interior)],
                load_sem.at[2 * halves + c],
            )
        )
    sep_loads = []
    for m in range(slots):
        for c in range(2):
            sep_loads.append(
                pltpu.make_async_copy(
                    sep_hbm.at[m, c],
                    sep2.at[m, :, pl.ds(c * sepw, sepw)],
                    sep_sem.at[2 * m + c],
                )
            )
    for copy in smalls + [load_src] + loads + cpl_loads:
        copy.start()

    @pl.when(s > 0)
    def _():
        greet(s - 1, fronts)

    greet(s, fronts - 1)

    @pl.when(s < last)
    def _():
        pl.semaphore_signal(barrier, inc=1, device_id=(s + 1, f), device_id_type=MESH)

    for copy in sep_loads:
        copy.start()

    zero_block = jnp.zeros((thin, LANES), BF16)
    run[cap] = jnp.zeros((thin, LANES), F32)
    for b in range(BATCHES):
        rblk[b, pieces] = zero_block
        vals[b, positions] = zero_block
        recv_b[b][cap] = zero_block
        recv_t[b, cap] = zero_block

    for copy in smalls + [load_src]:
        copy.wait()
    out_src, tag, back = leaf_tables(
        own_v[...], tgt_v[...], cnt_s[0, 0], parts, positions, fronts
    )
    leaf_tab[0:1, :] = out_src
    leaf_tab[1:2, :] = back
    leaf_tab[2:8, :] = jnp.zeros((6, LANES), I32)
    tag_v[...] = tag
    bring = pltpu.make_async_copy(leaf_tab, leaf_smem, smem_sem.at[0])
    bring.start()

    for h in range(halves):
        real = src_v[0, pl.ds(h * bnd, bnd), :]
        imag = src_v[1, pl.ds(h * bnd, bnd), :]
        top, low = pl.ds(2 * h * bnd, bnd), pl.ds((2 * h + 1) * bnd, bnd)
        packed = split_groups(real, imag)
        for g in range(GROUPS):
            xs[top, lane_sets[g]] = packed[g]
            xs[low, lane_sets[g]] = group_swap(packed[g])

    for copy in loads:
        copy.wait()
    base[...] = mm(leaf2[...], xs[...])
    for g in range(GROUPS):
        rounded = base[:, lane_sets[g]].astype(BF16)
        xb[pl.ds(0, interior), lane_sets[g]] = rounded
        xb[pl.ds(interior, interior), lane_sets[g]] = group_swap(rounded)
    for copy in cpl_loads:
        copy.wait()
    start_resid = mm(cpl2[...], xb[...])
    for g in range(GROUPS):
        pair = twins(start_resid[:, g * LANES : (g + 1) * LANES])
        resid0[2 * g], resid0[2 * g + 1] = pair
    bring.wait()

    has_next = jnp.where(s < last, fronts, 0)
    has_prev = jnp.where(s > 0, 1, 0)
    pl.semaphore_wait(barrier, fronts - 1 + has_next + has_prev)

    def push_tags():
        for to in peers(fronts - 1):
            pltpu.make_async_remote_copy(
                src_ref=tag_v,
                dst_ref=tag_recv.at[f],
                send_sem=tag_send,
                recv_sem=tag_arrive,
                device_id=(s, to),
                device_id_type=MESH,
            ).start()

    def send_blocks(source, target, send_sem, recv_sem, slab_to, count):
        for to in peers(count):
            pltpu.make_async_remote_copy(
                src_ref=source.at[pl.ds(2 * to, 2)],
                dst_ref=target.at[pl.ds(2 * f, 2)],
                send_sem=send_sem,
                recv_sem=recv_sem,
                device_id=(slab_to, to),
                device_id_type=MESH,
            ).start()

    def prev_copy(slab_to):
        return pltpu.make_async_remote_copy(
            src_ref=leaf_tab,
            dst_ref=prev_tab,
            send_sem=prev_send,
            recv_sem=prev_arrive,
            device_id=(slab_to, f),
            device_id_type=MESH,
        )

    def home_copy(slab_to):
        return pltpu.make_async_remote_copy(
            src_ref=inc,
            dst_ref=home,
            send_sem=home_send,
            recv_sem=home_arrive,
            device_id=(slab_to, f),
            device_id_type=MESH,
        )

    def await_bytes(buf, count, sem):
        view = buf.at[pl.ds(0, count)]
        pltpu.make_async_copy(view, view, sem).wait()

    def pack(value, count):
        block = value.astype(BF16).reshape(count, rows, LANES)
        upper, lower = block[:, :thin], block[:, thin:]
        return jnp.where(low_half(upper), upper, lower)

    def spread(block, put):
        for k, part in enumerate(twins(block)):
            put(0, k * thin, part)
            put(1, k * thin, twin_swap(part))

    def put_resid(b, resid):
        rblk[b, pl.ds(0, pieces)] = pack(resid, pieces)

    def push_resid(b):
        for i in range(cap):
            out_a[b, i] = rblk[b, leaf_smem[0, i]]
        send_blocks(out_a.at[b], recv_a[b], a_send.at[b], a_arrive.at[b], s, fronts - 1)
        for k in range(2):
            recv_a[b][2 * f + k] = out_a[b, 2 * f + k]

    def make_owner_tables():
        await_bytes(tag_recv, fronts - 1, tag_arrive)
        order, keep, ends, ret = owner_tables(tag_recv[:, 0, :], f, fronts)
        own_tab[0:1, :] = order
        own_tab[1:2, :] = keep
        own_tab[2:3, :] = ends
        own_tab[3:4, :] = ret
        own_tab[4:8, :] = jnp.zeros((4, LANES), I32)
        bring = pltpu.make_async_copy(own_tab, own_smem, smem_sem.at[1])
        bring.start()
        bring.wait()

    tag_recv[f] = tag_v[...]

    push_tags()

    @pl.when(s > 0)
    def _():
        @pl.when(s < last)
        def _():
            prev_copy(s + 1).start()

        near = leaf2[:, pl.ds(0, 2 * bnd)]
        left = mm(cpl2[:, pl.ds(0, interior)], near)
        right = mm(cpl2[:, pl.ds(interior, interior)], near)
        comp2[:, pl.ds(0, bnd)] = (left[:, :bnd] - right[:, bnd:]).astype(BF16)
        comp2[:, pl.ds(bnd, bnd)] = (left[:, bnd:] + right[:, :bnd]).astype(BF16)
        prev_copy(s).wait_recv()
        bring = pltpu.make_async_copy(prev_tab, prev_smem, smem_sem.at[0])
        bring.start()
        bring.wait()
        make_owner_tables()

    for b in range(BATCHES):

        @pl.when(s > 0)
        def _():
            await_bytes(recv_b[b], cap, b_arrive.at[b])
            for p in range(pieces):

                def put(which, offset, part):
                    xtwin[b, pl.ds(which * bnd + p * rows + offset, thin), :] = part

                spread(recv_b[b][prev_smem[1, p]], put)
            put_resid(b, resid0[b] + mm(comp2[...], xtwin[b]))

        @pl.when(s == 0)
        def _():
            put_resid(b, resid0[b])

        push_resid(b)
    @pl.when(s == 0)
    def _():
        prev_copy(s + 1).start()
        make_owner_tables()

    @pl.when(s > 0)
    def _():
        for g in range(GROUPS):
            even, odd = xtwin[2 * g], xtwin[2 * g + 1]
            xin[:, lane_sets[g]] = jnp.where(low_half(even), even, odd)
        real, imag = join_groups(xin[pl.ds(0, bnd), lane_sets[0]], xin[pl.ds(0, bnd), lane_sets[1]])
        inc[:, 0] = real.reshape(pieces, rows, LANES)
        inc[:, 1] = imag.reshape(pieces, rows, LANES)
        home_copy(s - 1).start()

    def put_solution(full):
        full = full.astype(BF16)
        sol_ref[0], sol_ref[1] = join_groups(full[:, :LANES], full[:, LANES:])

    for copy in sep_loads:
        copy.wait()

    for b in range(BATCHES):
        await_bytes(recv_a[b], cap - 2, a_arrive.at[b])
        running = jnp.zeros((thin, LANES), F32)
        for i in range(cap):
            block = recv_a[b][own_smem[0, i]].astype(F32)
            running = jnp.where(own_smem[1, i] > 0, running, 0.0) + block
            run[i] = running
        for m in range(slots):
            for q in range(parts):

                def put(which, offset, part):
                    xsep[m, pl.ds(which * sepw + q * rows + offset, thin), :] = part

                spread(run[own_smem[2, m * parts + q]].astype(BF16), put)
        for m in range(slots):
            vals[b, pl.ds(m * parts, parts)] = pack(mm(sep2[m], xsep[m]), parts)
        for i in range(cap):
            out_b[b, i] = vals[b, own_smem[3, i]]

        @pl.when(s < last)
        def _():
            send_blocks(
                out_b.at[b], recv_b[b], b_send.at[b], b_arrive.at[b], s + 1, fronts
            )

        @pl.when(s == last)
        def _():
            send_blocks(
                out_b.at[b], recv_t.at[b], b_send.at[b], t_arrive.at[b], s, fronts - 1
            )
            for k in range(2):
                recv_t[b, 2 * f + k] = out_b[b, 2 * f + k]

    @pl.when(s == 0)
    def _():
        put_solution(base[...])

    @pl.when(s > 0)
    def _():
        put_solution(base[...] + mm(leaf2[:, pl.ds(0, 2 * bnd)], xin[...]))

    @pl.when(s < last)
    def _():
        home_copy(s).wait_recv()
        trace_ref[...] = home[...]
        for b in range(BATCHES):
            await_bytes(out_b.at[b], cap, b_send.at[b])
        prev_copy(s).wait_send()

    @pl.when(s == last)
    def _():
        for b in range(BATCHES):
            await_bytes(recv_t.at[b], cap - 2, t_arrive.at[b])
        for p in range(pieces):
            at = leaf_smem[1, p]
            pairs = [twins(recv_t[b, at]) for b in range(BATCHES)]
            for k in range(2):
                low = low_half(pairs[0][k])
                real, imag = join_groups(
                    jnp.where(low, pairs[0][k], pairs[1][k]),
                    jnp.where(low, pairs[2][k], pairs[3][k]),
                )
                trace_ref[p, 0, pl.ds(k * thin, thin), :] = real
                trace_ref[p, 1, pl.ds(k * thin, thin), :] = imag
        for b in range(BATCHES):
            await_bytes(out_b.at[b], cap - 2, b_send.at[b])

    @pl.when(s > 0)
    def _():
        home_copy(s).wait_send()

    for b in range(BATCHES):
        await_bytes(out_a.at[b], cap - 2, a_send.at[b])
    await_bytes(tag_recv, fronts - 1, tag_send)


def solution(mesh):
    slabs, fronts = mesh.shape["slab"], mesh.shape["front"]
    ring = 4

    def body(source, leaf_inverse, boundary_map, sep_inverse, owner_map, piece_count, piece_target):
        src = source[0, 0]
        inv = leaf_inverse[0, 0]
        cpl = boundary_map[0, 0]
        sep = sep_inverse[0]
        interior, cols = src.shape[1], src.shape[2]
        bnd = cpl.shape[1]
        seps, pieces = owner_map.shape[1], piece_target.shape[2]
        rows = bnd // pieces
        slots, sepw = sep.shape[0], sep.shape[2]
        positions = slots * (sepw // rows)
        cap = 2 * fronts
        halves = interior // bnd

        def blocks(count):
            return pltpu.VMEM((BATCHES, count, rows // 2, LANES), BF16)

        def single(count):
            return pltpu.VMEM((count, rows // 2, LANES), BF16)

        vmem = pl.BlockSpec(memory_space=pltpu.VMEM)
        anyspace = pl.BlockSpec(memory_space=pltpu.HBM)
        dma = pltpu.SemaphoreType.DMA
        table = pltpu.VMEM((8, LANES), I32)
        smem_table = pltpu.SMEM((8, LANES), I32)
        solved, trace = pl.pallas_call(
            functools.partial(sweep_kernel, slabs, fronts, ring),
            out_shape=(
                jax.ShapeDtypeStruct((2, interior, cols), BF16),
                jax.ShapeDtypeStruct((pieces, 2, rows, cols), BF16),
            ),
            in_specs=[anyspace] * 5 + [pl.BlockSpec(memory_space=pl.ANY), anyspace],
            out_specs=(vmem, vmem),
            scratch_shapes=[
                pltpu.VMEM((2, interior, cols), BF16),
                pltpu.VMEM((1, seps), I32),
                pltpu.VMEM((1, pieces), I32),
                pltpu.SMEM((1, 1), I32),
                pltpu.VMEM((interior, 2 * interior), BF16),
                pltpu.VMEM((bnd, 2 * interior), BF16),
                pltpu.VMEM((slots, sepw, 2 * sepw), BF16),
                pltpu.VMEM((bnd, 2 * bnd), BF16),
                pltpu.VMEM((2 * interior, 2 * cols), BF16),
                pltpu.VMEM((2 * interior, 2 * cols), BF16),
                pltpu.VMEM((2 * bnd, 2 * cols), BF16),
                pltpu.VMEM((BATCHES, 2 * bnd, LANES), BF16),
                pltpu.VMEM((slots, 2 * sepw, LANES), BF16),
                pltpu.VMEM((interior, 2 * cols), F32),
                pltpu.VMEM((BATCHES, bnd, LANES), F32),
                blocks(pieces + 1),
                pltpu.VMEM((pieces, 2, rows, cols), BF16),
                blocks(cap),
                single(cap),
                single(cap),
                single(cap),
                single(cap),
                pltpu.VMEM((cap + 1, rows // 2, LANES), F32),
                blocks(positions + 1),
                blocks(cap),
                single(cap + 1),
                single(cap + 1),
                single(cap + 1),
                single(cap + 1),
                blocks(cap + 1),
                pltpu.VMEM((pieces, 2, rows, cols), BF16),
                pltpu.VMEM((1, LANES), I32),
                pltpu.VMEM((fronts, 1, LANES), I32),
                table,
                table,
                table,
                smem_table,
                smem_table,
                smem_table,
                dma((4,)),
                dma((2 * halves + 2,)),
                dma((2 * slots,)),
                dma,
                dma,
                dma,
                dma,
                dma((BATCHES,)),
                dma((BATCHES,)),
                dma((BATCHES,)),
                dma((BATCHES,)),
                dma((BATCHES,)),
                dma,
                dma,
                dma((2,)),
            ],
            compiler_params=pltpu.CompilerParams(
                collective_id=0, has_side_effects=True, vmem_limit_bytes=40 * 1024 * 1024
            ),
        )(stay(src), stay(inv), stay(cpl), stay(sep), stay(owner_map), piece_count, stay(piece_target[0]))
        return solved[None, None], trace[None, None]

    return jax.shard_map(
        body,
        mesh=mesh,
        in_specs=(
            P("slab", "front", None, None, None),
            P("slab", "front", None, None, None),
            P("slab", "front", None, None, None),
            P("slab", "front", None, None, None),
            P("slab", None),
            P("slab", "front"),
            P("slab", "front", None),
        ),
        out_specs=(
            P("slab", "front", None, None, None),
            P("slab", "front", None, None, None, None),
        ),
        check_vma=False,
    )
```

```python
import functools

import jax
import jax.numpy as jnp
from jax import lax
from jax.experimental import pallas as pl
from jax.experimental.pallas import tpu as pltpu
from jax.sharding import PartitionSpec as P

MESH = pl.DeviceIdType.MESH
BF16 = jnp.bfloat16
F32 = jnp.float32
I32 = jnp.int32
LANES = 128
HALF = LANES // 2
QUARTER = LANES // 4
BATCHES = 4
GROUPS = 2


def mm(a, b):
    return jnp.dot(a, b, preferred_element_type=F32)


def turn(x, distance=HALF):
    return pltpu.roll(x, distance, 1)


def iota(shape, axis):
    return lax.broadcasted_iota(I32, shape, axis)


def low_half(x):
    return iota(x.shape, len(x.shape) - 1) < HALF


def quarters(a, b, c, d):
    lane = iota(a.shape, 1)
    front = jnp.where(lane < QUARTER, a, b)
    return jnp.where(lane < HALF, front, jnp.where(lane < HALF + QUARTER, c, d))


def group_swap(x):
    left, right = turn(x, LANES - QUARTER), turn(x, QUARTER)
    return jnp.where(iota(x.shape, 1) % HALF < QUARTER, -left, right)


def twin_swap(x):
    moved = turn(x, QUARTER)
    return jnp.where(iota(x.shape, 1) % HALF < QUARTER, -moved, moved)


def twins(x):
    turned, low = turn(x), low_half(x)
    return jnp.where(low, x, turned), jnp.where(low, turned, x)


def split_groups(real, imag):
    left, right = LANES - QUARTER, QUARTER
    return (
        quarters(real, turn(imag, right), turn(real, right), turn(imag)),
        quarters(turn(real), turn(imag, left), turn(real, left), imag),
    )


def join_groups(g0, g1):
    left, right = LANES - QUARTER, QUARTER
    g0_left, g1_right = turn(g0, left), turn(g1, right)
    return (
        quarters(g0, g0_left, turn(g1), g1_right),
        quarters(g0_left, turn(g0), g1_right, g1),
    )


def total(mask, value, axis):
    return jnp.sum(jnp.where(mask, value, 0), axis=axis, keepdims=True)


def as_column(row_value, size):
    shape = (size, size)
    return total(iota(shape, 0) == iota(shape, 1), row_value, 1)


def as_row(column, size):
    shape = (size, LANES)
    return total(iota(shape, 0) == iota(shape, 1), column, 0)


def leaf_tables(owners, targets, count, parts, positions, fronts):
    seps, pieces = owners.shape[1], targets.shape[1]
    square = (seps, seps)
    owner_col = as_column(owners, seps)
    slot_row = total((owner_col == owners) & (iota(square, 0) < iota(square, 1)), 1, 0)
    target_col = as_column(targets, pieces)
    wide = (pieces, seps)
    sep_id = iota(wide, 1)
    match = (target_col >= sep_id * parts) & (target_col < sep_id * parts + parts)
    destination = total(match, owners, 1)
    position = total(match, (slot_row - sep_id) * parts, 1) + target_col
    small = (pieces, pieces)
    piece_col, piece_row = iota(small, 0), iota(small, 1)
    destination_row = total(piece_col == piece_row, destination, 0)
    before = (destination == destination_row) & (piece_row < count) & (piece_row < piece_col)
    index = destination * 2 + total(before, 1, 1)
    shape = (pieces, LANES)
    piece_id, lane = iota(shape, 0), iota(shape, 1)
    usable = piece_id < count
    route = (lane == index) & usable
    out_src = total(route, piece_id - pieces, 0) + pieces
    tag = total(route, position - positions, 0) + positions
    back = total(piece_id == lane, jnp.where(usable, index, 2 * fronts), 0)
    return out_src, tag, back


def owner_tables(tags, f, fronts):
    cap = 2 * fronts
    lane, row = iota((fronts, LANES), 1), iota((fronts, LANES), 0)
    first = total(lane == 2 * f, tags, 1)
    second = total(lane == 2 * f + 1, tags, 1)
    picked = jnp.where(lane % 2 == 0, first, second)
    back = total(row == lane // 2, picked, 0)
    col = jnp.concatenate([first, second], axis=0)
    lane, row = iota((cap, LANES), 1), iota((cap, LANES), 0)
    tag_row = as_row(col, cap)
    valid = lane < cap
    same = valid & (tag_row == col) & (lane < row)
    rank = total(same | (valid & (tag_row < col)), 1, 1)
    repeat = jnp.max(jnp.where(same, 1, 0), axis=1, keepdims=True)
    placed = rank == lane
    order = total(placed, row % fronts * 2 + row // fronts, 0)
    keep = total(placed, repeat, 0)
    upto = total(col <= lane, 1, 0)
    hit = total(col == lane, 1, 0)
    ends = jnp.where(hit > 0, upto - 1, cap)
    return order, keep, ends, back


def stay(x):
    return pltpu.with_memory_space_constraint(x, pltpu.HBM)


def around(size):
    half = size // 2
    return [half + (1 - 2 * (j % 2)) * ((j + 1) // 2) for j in range(size)]


def ordered_offsets(depth, ring):
    offsets = [(dz, dx) for dx in around(ring) for dz in around(depth)]
    return sorted(offsets, key=lambda o: -min(o[0], depth - o[0]) - min(o[1], ring - o[1]))


def sweep_kernel(
    slabs,
    fronts,
    ring,
    src_hbm,
    inv_hbm,
    cpl_hbm,
    sep_hbm,
    own_hbm,
    cnt_hbm,
    tgt_hbm,
    sol_ref,
    trace_ref,
    src_v,
    own_v,
    tgt_v,
    cnt_s,
    leaf2,
    cpl2,
    sep2,
    comp2,
    xs,
    xb,
    xin,
    xtwin,
    xsep,
    base,
    resid0,
    rblk,
    inc,
    out_a,
    recv_a0,
    recv_a1,
    recv_a2,
    recv_a3,
    run,
    vals,
    out_b,
    recv_b0,
    recv_b1,
    recv_b2,
    recv_b3,
    recv_t,
    home,
    tag_v,
    tag_recv,
    leaf_tab,
    prev_tab,
    own_tab,
    leaf_smem,
    prev_smem,
    own_smem,
    small_sem,
    load_sem,
    sep_sem,
    tag_send,
    tag_arrive,
    prev_send,
    prev_arrive,
    a_send,
    a_arrive,
    b_send,
    b_arrive,
    t_arrive,
    home_send,
    home_arrive,
    smem_sem,
):
    s = lax.axis_index("slab")
    f = lax.axis_index("front")
    last = slabs - 1
    interior = src_v.shape[1]
    bnd = cpl2.shape[0]
    slots, sepw = sep2.shape[0], sep2.shape[1]
    pieces = inc.shape[0]
    rows = inc.shape[2]
    thin = rows // 2
    parts = sepw // rows
    positions = slots * parts
    cap = 2 * fronts
    halves = interior // bnd
    depth = fronts // ring
    recv_a = (recv_a0, recv_a1, recv_a2, recv_a3)
    recv_b = (recv_b0, recv_b1, recv_b2, recv_b3)
    lane_sets = [pl.ds(b * LANES, LANES) for b in range(GROUPS)]

    f_z, f_x = lax.div(f, ring), lax.rem(f, ring)
    z_of = [lax.rem(f_z + dz, depth) * ring for dz in range(depth)]
    x_of = [lax.rem(f_x + dx, ring) for dx in range(ring)]

    def peers(count):
        for dz, dx in ordered_offsets(depth, ring)[:count]:
            yield z_of[dz] + x_of[dx]

    barrier = pltpu.get_barrier_semaphore()

    def greet(slab_to, count):
        for to in peers(count):
            pl.semaphore_signal(barrier, inc=1, device_id=(slab_to, to), device_id_type=MESH)

    smalls = [
        pltpu.make_async_copy(own_hbm, own_v, small_sem.at[0]),
        pltpu.make_async_copy(tgt_hbm, tgt_v, small_sem.at[1]),
        pltpu.make_async_copy(cnt_hbm, cnt_s, small_sem.at[2]),
    ]
    load_src = pltpu.make_async_copy(src_hbm, src_v, small_sem.at[3])
    loads = []
    for h in range(halves):
        for c in range(2):
            at = (2 * h + c) * bnd
            loads.append(
                pltpu.make_async_copy(
                    inv_hbm.at[c, :, pl.ds(h * bnd, bnd)],
                    leaf2.at[:, pl.ds(at, bnd)],
                    load_sem.at[2 * h + c],
                )
            )
    cpl_loads = []
    for c in range(2):
        cpl_loads.append(
            pltpu.make_async_copy(
                cpl_hbm.at[c],
                cpl2.at[:, pl.ds(c * interior, interior)],
                load_sem.at[2 * halves + c],
            )
        )
    sep_loads = []
    for m in range(slots):
        for c in range(2):
            sep_loads.append(
                pltpu.make_async_copy(
                    sep_hbm.at[m, c],
                    sep2.at[m, :, pl.ds(c * sepw, sepw)],
                    sep_sem.at[2 * m + c],
                )
            )
    for copy in smalls + [load_src] + loads + cpl_loads:
        copy.start()

    @pl.when(s > 0)
    def _():
        greet(s - 1, fronts)

    greet(s, fronts - 1)

    @pl.when(s < last)
    def _():
        pl.semaphore_signal(barrier, inc=1, device_id=(s + 1, f), device_id_type=MESH)

    for copy in sep_loads:
        copy.start()

    zero_block = jnp.zeros((thin, LANES), BF16)
    run[cap] = jnp.zeros((thin, LANES), F32)
    for b in range(BATCHES):
        rblk[b, pieces] = zero_block
        vals[b, positions] = zero_block
        recv_b[b][cap] = zero_block
        recv_t[b, cap] = zero_block

    for copy in smalls + [load_src]:
        copy.wait()
    out_src, tag, back = leaf_tables(
        own_v[...], tgt_v[...], cnt_s[0, 0], parts, positions, fronts
    )
    leaf_tab[0:1, :] = out_src
    leaf_tab[1:2, :] = back
    leaf_tab[2:8, :] = jnp.zeros((6, LANES), I32)
    tag_v[...] = tag
    bring = pltpu.make_async_copy(leaf_tab, leaf_smem, smem_sem.at[0])
    bring.start()

    for h in range(halves):
        real = src_v[0, pl.ds(h * bnd, bnd), :]
        imag = src_v[1, pl.ds(h * bnd, bnd), :]
        top, low = pl.ds(2 * h * bnd, bnd), pl.ds((2 * h + 1) * bnd, bnd)
        packed = split_groups(real, imag)
        for g in range(GROUPS):
            xs[top, lane_sets[g]] = packed[g]
            xs[low, lane_sets[g]] = group_swap(packed[g])

    for copy in loads:
        copy.wait()
    base[...] = mm(leaf2[...], xs[...])
    for g in range(GROUPS):
        rounded = base[:, lane_sets[g]].astype(BF16)
        xb[pl.ds(0, interior), lane_sets[g]] = rounded
        xb[pl.ds(interior, interior), lane_sets[g]] = group_swap(rounded)
    for copy in cpl_loads:
        copy.wait()
    start_resid = mm(cpl2[...], xb[...])
    for g in range(GROUPS):
        pair = twins(start_resid[:, g * LANES : (g + 1) * LANES])
        resid0[2 * g], resid0[2 * g + 1] = pair
    bring.wait()

    has_next = jnp.where(s < last, fronts, 0)
    has_prev = jnp.where(s > 0, 1, 0)
    pl.semaphore_wait(barrier, fronts - 1 + has_next + has_prev)

    def push_tags():
        for to in peers(fronts - 1):
            pltpu.make_async_remote_copy(
                src_ref=tag_v,
                dst_ref=tag_recv.at[f],
                send_sem=tag_send,
                recv_sem=tag_arrive,
                device_id=(s, to),
                device_id_type=MESH,
            ).start()

    def send_blocks(source, target, send_sem, recv_sem, slab_to, count):
        for to in peers(count):
            pltpu.make_async_remote_copy(
                src_ref=source.at[pl.ds(2 * to, 2)],
                dst_ref=target.at[pl.ds(2 * f, 2)],
                send_sem=send_sem,
                recv_sem=recv_sem,
                device_id=(slab_to, to),
                device_id_type=MESH,
            ).start()

    def prev_copy(slab_to):
        return pltpu.make_async_remote_copy(
            src_ref=leaf_tab,
            dst_ref=prev_tab,
            send_sem=prev_send,
            recv_sem=prev_arrive,
            device_id=(slab_to, f),
            device_id_type=MESH,
        )

    def home_copy(slab_to):
        return pltpu.make_async_remote_copy(
            src_ref=inc,
            dst_ref=home,
            send_sem=home_send,
            recv_sem=home_arrive,
            device_id=(slab_to, f),
            device_id_type=MESH,
        )

    def await_bytes(buf, count, sem):
        view = buf.at[pl.ds(0, count)]
        pltpu.make_async_copy(view, view, sem).wait()

    def pack(value, count):
        block = value.astype(BF16).reshape(count, rows, LANES)
        upper, lower = block[:, :thin], block[:, thin:]
        return jnp.where(low_half(upper), upper, lower)

    def spread(block, put):
        for k, part in enumerate(twins(block)):
            put(0, k * thin, part)
            put(1, k * thin, twin_swap(part))

    def put_resid(b, resid):
        rblk[b, pl.ds(0, pieces)] = pack(resid, pieces)

    def push_resid(b):
        for i in range(cap):
            out_a[b, i] = rblk[b, leaf_smem[0, i]]
        send_blocks(out_a.at[b], recv_a[b], a_send.at[b], a_arrive.at[b], s, fronts - 1)
        for k in range(2):
            recv_a[b][2 * f + k] = out_a[b, 2 * f + k]

    def make_owner_tables():
        await_bytes(tag_recv, fronts - 1, tag_arrive)
        order, keep, ends, ret = owner_tables(tag_recv[:, 0, :], f, fronts)
        own_tab[0:1, :] = order
        own_tab[1:2, :] = keep
        own_tab[2:3, :] = ends
        own_tab[3:4, :] = ret
        own_tab[4:8, :] = jnp.zeros((4, LANES), I32)
        bring = pltpu.make_async_copy(own_tab, own_smem, smem_sem.at[1])
        bring.start()
        bring.wait()

    tag_recv[f] = tag_v[...]

    push_tags()

    @pl.when(s > 0)
    def _():
        @pl.when(s < last)
        def _():
            prev_copy(s + 1).start()

        near = leaf2[:, pl.ds(0, 2 * bnd)]
        left = mm(cpl2[:, pl.ds(0, interior)], near)
        right = mm(cpl2[:, pl.ds(interior, interior)], near)
        comp2[:, pl.ds(0, bnd)] = (left[:, :bnd] - right[:, bnd:]).astype(BF16)
        comp2[:, pl.ds(bnd, bnd)] = (left[:, bnd:] + right[:, :bnd]).astype(BF16)
        prev_copy(s).wait_recv()
        bring = pltpu.make_async_copy(prev_tab, prev_smem, smem_sem.at[0])
        bring.start()
        bring.wait()
        make_owner_tables()

    for b in range(BATCHES):

        @pl.when(s > 0)
        def _():
            await_bytes(recv_b[b], cap, b_arrive.at[b])
            for p in range(pieces):

                def put(which, offset, part):
                    xtwin[b, pl.ds(which * bnd + p * rows + offset, thin), :] = part

                spread(recv_b[b][prev_smem[1, p]], put)
            put_resid(b, resid0[b] + mm(comp2[...], xtwin[b]))

        @pl.when(s == 0)
        def _():
            put_resid(b, resid0[b])

        push_resid(b)
    @pl.when(s == 0)
    def _():
        prev_copy(s + 1).start()
        make_owner_tables()

    @pl.when(s > 0)
    def _():
        for g in range(GROUPS):
            even, odd = xtwin[2 * g], xtwin[2 * g + 1]
            xin[:, lane_sets[g]] = jnp.where(low_half(even), even, odd)
        real, imag = join_groups(xin[pl.ds(0, bnd), lane_sets[0]], xin[pl.ds(0, bnd), lane_sets[1]])
        inc[:, 0] = real.reshape(pieces, rows, LANES)
        inc[:, 1] = imag.reshape(pieces, rows, LANES)
        home_copy(s - 1).start()

    def put_solution(full):
        full = full.astype(BF16)
        sol_ref[0], sol_ref[1] = join_groups(full[:, :LANES], full[:, LANES:])

    for copy in sep_loads:
        copy.wait()

    for b in range(BATCHES):
        await_bytes(recv_a[b], cap - 2, a_arrive.at[b])
        running = jnp.zeros((thin, LANES), F32)
        for i in range(cap):
            block = recv_a[b][own_smem[0, i]].astype(F32)
            running = jnp.where(own_smem[1, i] > 0, running, 0.0) + block
            run[i] = running
        for m in range(slots):
            for q in range(parts):

                def put(which, offset, part):
                    xsep[m, pl.ds(which * sepw + q * rows + offset, thin), :] = part

                spread(run[own_smem[2, m * parts + q]].astype(BF16), put)
        for m in range(slots):
            vals[b, pl.ds(m * parts, parts)] = pack(mm(sep2[m], xsep[m]), parts)
        for i in range(cap):
            out_b[b, i] = vals[b, own_smem[3, i]]

        @pl.when(s < last)
        def _():
            send_blocks(
                out_b.at[b], recv_b[b], b_send.at[b], b_arrive.at[b], s + 1, fronts
            )

        @pl.when(s == last)
        def _():
            send_blocks(
                out_b.at[b], recv_t.at[b], b_send.at[b], t_arrive.at[b], s, fronts - 1
            )
            for k in range(2):
                recv_t[b, 2 * f + k] = out_b[b, 2 * f + k]

    @pl.when(s == 0)
    def _():
        put_solution(base[...])

    @pl.when(s > 0)
    def _():
        put_solution(base[...] + mm(leaf2[:, pl.ds(0, 2 * bnd)], xin[...]))

    @pl.when(s < last)
    def _():
        home_copy(s).wait_recv()
        trace_ref[...] = home[...]
        for b in range(BATCHES):
            await_bytes(out_b.at[b], cap, b_send.at[b])
        prev_copy(s).wait_send()

    @pl.when(s == last)
    def _():
        for b in range(BATCHES):
            await_bytes(recv_t.at[b], cap - 2, t_arrive.at[b])
        for p in range(pieces):
            at = leaf_smem[1, p]
            pairs = [twins(recv_t[b, at]) for b in range(BATCHES)]
            for k in range(2):
                low = low_half(pairs[0][k])
                real, imag = join_groups(
                    jnp.where(low, pairs[0][k], pairs[1][k]),
                    jnp.where(low, pairs[2][k], pairs[3][k]),
                )
                trace_ref[p, 0, pl.ds(k * thin, thin), :] = real
                trace_ref[p, 1, pl.ds(k * thin, thin), :] = imag
        for b in range(BATCHES):
            await_bytes(out_b.at[b], cap - 2, b_send.at[b])

    @pl.when(s > 0)
    def _():
        home_copy(s).wait_send()

    for b in range(BATCHES):
        await_bytes(out_a.at[b], cap - 2, a_send.at[b])
    await_bytes(tag_recv, fronts - 1, tag_send)


def solution(mesh):
    slabs, fronts = mesh.shape["slab"], mesh.shape["front"]
    ring = 4

    def body(source, leaf_inverse, boundary_map, sep_inverse, owner_map, piece_count, piece_target):
        src = source[0, 0]
        inv = leaf_inverse[0, 0]
        cpl = boundary_map[0, 0]
        sep = sep_inverse[0]
        interior, cols = src.shape[1], src.shape[2]
        bnd = cpl.shape[1]
        seps, pieces = owner_map.shape[1], piece_target.shape[2]
        rows = bnd // pieces
        slots, sepw = sep.shape[0], sep.shape[2]
        positions = slots * (sepw // rows)
        cap = 2 * fronts
        halves = interior // bnd

        def blocks(count):
            return pltpu.VMEM((BATCHES, count, rows // 2, LANES), BF16)

        def single(count):
            return pltpu.VMEM((count, rows // 2, LANES), BF16)

        vmem = pl.BlockSpec(memory_space=pltpu.VMEM)
        anyspace = pl.BlockSpec(memory_space=pltpu.HBM)
        dma = pltpu.SemaphoreType.DMA
        table = pltpu.VMEM((8, LANES), I32)
        smem_table = pltpu.SMEM((8, LANES), I32)
        solved, trace = pl.pallas_call(
            functools.partial(sweep_kernel, slabs, fronts, ring),
            out_shape=(
                jax.ShapeDtypeStruct((2, interior, cols), BF16),
                jax.ShapeDtypeStruct((pieces, 2, rows, cols), BF16),
            ),
            in_specs=[anyspace] * 5 + [pl.BlockSpec(memory_space=pl.ANY), anyspace],
            out_specs=(vmem, vmem),
            scratch_shapes=[
                pltpu.VMEM((2, interior, cols), BF16),
                pltpu.VMEM((1, seps), I32),
                pltpu.VMEM((1, pieces), I32),
                pltpu.SMEM((1, 1), I32),
                pltpu.VMEM((interior, 2 * interior), BF16),
                pltpu.VMEM((bnd, 2 * interior), BF16),
                pltpu.VMEM((slots, sepw, 2 * sepw), BF16),
                pltpu.VMEM((bnd, 2 * bnd), BF16),
                pltpu.VMEM((2 * interior, 2 * cols), BF16),
                pltpu.VMEM((2 * interior, 2 * cols), BF16),
                pltpu.VMEM((2 * bnd, 2 * cols), BF16),
                pltpu.VMEM((BATCHES, 2 * bnd, LANES), BF16),
                pltpu.VMEM((slots, 2 * sepw, LANES), BF16),
                pltpu.VMEM((interior, 2 * cols), F32),
                pltpu.VMEM((BATCHES, bnd, LANES), F32),
                blocks(pieces + 1),
                pltpu.VMEM((pieces, 2, rows, cols), BF16),
                blocks(cap),
                single(cap),
                single(cap),
                single(cap),
                single(cap),
                pltpu.VMEM((cap + 1, rows // 2, LANES), F32),
                blocks(positions + 1),
                blocks(cap),
                single(cap + 1),
                single(cap + 1),
                single(cap + 1),
                single(cap + 1),
                blocks(cap + 1),
                pltpu.VMEM((pieces, 2, rows, cols), BF16),
                pltpu.VMEM((1, LANES), I32),
                pltpu.VMEM((fronts, 1, LANES), I32),
                table,
                table,
                table,
                smem_table,
                smem_table,
                smem_table,
                dma((4,)),
                dma((2 * halves + 2,)),
                dma((2 * slots,)),
                dma,
                dma,
                dma,
                dma,
                dma((BATCHES,)),
                dma((BATCHES,)),
                dma((BATCHES,)),
                dma((BATCHES,)),
                dma((BATCHES,)),
                dma,
                dma,
                dma((2,)),
            ],
            compiler_params=pltpu.CompilerParams(
                collective_id=0, has_side_effects=True, vmem_limit_bytes=40 * 1024 * 1024
            ),
        )(stay(src), stay(inv), stay(cpl), stay(sep), stay(owner_map), piece_count, stay(piece_target[0]))
        return solved[None, None], trace[None, None]

    return jax.shard_map(
        body,
        mesh=mesh,
        in_specs=(
            P("slab", "front", None, None, None),
            P("slab", "front", None, None, None),
            P("slab", "front", None, None, None),
            P("slab", "front", None, None, None),
            P("slab", None),
            P("slab", "front"),
            P("slab", "front", None),
        ),
        out_specs=(
            P("slab", "front", None, None, None),
            P("slab", "front", None, None, None, None),
        ),
        check_vma=False,
    )
```
